32 devices in a mesh: seq: 16 (over z, y, x), head: 2 (over core).
Axes of the slice: x: 2, y: 2, z: 4, core: 2. Of those that a mesh axis runs over, the one named last changes fastest.
Arguments:
- query_raw: bfloat16 [2048, 2048], P('seq', 'head'), may hold values from -6 to 6
- key_raw: bfloat16 [2048, 2048], P('seq', 'head'), may hold values from -6 to 6
- value_raw: bfloat16 [2048, 2048], P('seq', 'head'), may hold values from -6 to 6
- gate_raw: float32 [2048, 2048], P('seq', 'head')
- beta_raw: float32 [2048, 16], P('seq', 'head'), may hold values from -8.5 to 3.5
- conv_weight: float32 [3, 4, 2048], P(None, None, 'head'), may hold values from -3 to 3
- decay_log: float32 [2048], P('head')
- grad_out: bfloat16 [2048, 2048], P('seq', 'head'), may hold values from -6 to 6
Outputs:
- query_grad: bfloat16 [2048, 2048], P('seq', 'head')
- key_grad: bfloat16 [2048, 2048], P('seq', 'head')
- value_grad: bfloat16 [2048, 2048], P('seq', 'head')
- gate_grad: float32 [2048, 2048], P('seq', 'head')
- beta_grad: float32 [2048, 16], P('seq', 'head')
- conv_grad: float32 [3, 4, 2048], P(None, None, 'head')
- decay_grad: float32 [2048], P('head')
The draws below stay inside these ranges and needn't reach their ends.
All inputs are finite; a program needn't handle non-finite values.
Results may differ from the reference program's by a relative error of at most 0.0018.
Values may be sent and summed in bfloat16 or wider, within the bound.
A program may use at most 128 MiB of HBM per device.

```python
import jax
import jax.numpy as jnp
from jax import lax

HEADS = 16
DK = 128
KCONV = 4
TOK_DEV = 128
TOKENS = 2048
CH = 2048


def gate_parts(key):
    base = jax.random.fold_in(key, 7)
    pick_key, fast_key, slow_key, normal_key, spot_key, loss_key = jax.random.split(base, 6)
    channels = HEADS * DK
    share = 0.5
    slow = jax.random.uniform(pick_key, (channels,)) < share
    fast_speed = jnp.exp(jax.random.uniform(fast_key, (channels,), minval=jnp.log(1.0 / 50.0), maxval=jnp.log(1.0 / 30.0)))
    slow_speed = jnp.log(10.0) / TOKENS * jnp.exp(jax.random.uniform(slow_key, (channels,), minval=jnp.log(0.02), maxval=jnp.log(0.2)))
    speed = jnp.where(slow, slow_speed, fast_speed)
    decay_values = jnp.log(speed / 0.8)
    score_logits = jnp.clip(jax.random.normal(normal_key, (TOKENS, channels)), -3.0, 3.0)
    spots = jax.random.randint(spot_key, (3,), 0, TOKENS)
    losses = jax.random.uniform(loss_key, (channels,), minval=0.22, maxval=0.5)
    target_value = losses / (speed / 0.8)
    spike_amount = target_value + jnp.log(-jnp.expm1(-target_value))
    positions = jnp.arange(TOKENS)
    flagged_entries = jnp.any(positions[:, None] == spots[None, :], axis=1)
    score_logits = jnp.where(flagged_entries[:, None], spike_amount[None, :], score_logits)
    return (decay_values.astype(jnp.float32), score_logits.astype(jnp.float32))


def draw_decay_log(key, part):
    return gate_parts(key)[0]


def draw_gate_raw(key, part):
    return gate_parts(key)[1]


def draw_beta_raw(key, part):
    center_key, noise_key = jax.random.split(jax.random.fold_in(key, 3))
    centers = jax.random.uniform(center_key, (HEADS,), minval=-6.0, maxval=1.0)
    noise = jnp.clip(jax.random.normal(noise_key, (TOKENS, HEADS)), -2.5, 2.5) * 0.8
    return (centers[None, :] + noise).astype(jnp.float32)


def block_scale(rng, dims, cuts, low, largest):
    def one(axis_at, parts):
        heights = jax.random.uniform(jax.random.fold_in(jax.random.fold_in(rng, 6), axis_at), (parts,), jnp.float32, low / len(cuts), largest / len(cuts))
        return jnp.repeat(jnp.exp(heights), dims[axis_at] // parts).reshape((-1,) + (1,) * (len(dims) - axis_at - 1))

    loudness = one(*cuts[0])
    for cut in cuts[1:]:
        loudness = loudness * one(*cut)
    return loudness


def centred(rng, dims, deviation, limit, shards=(), held_as=jnp.bfloat16):
    result = jax.random.normal(rng, dims, jnp.float32) * deviation
    if len(shards) > 0:
        result = block_scale(rng, dims, shards, -0.22, 0.18) * result
    return jnp.clip(result, min=-limit, max=limit).astype(held_as)


def setup_inputs(seed: int = 0) -> dict:
    arg_keys = jax.random.split(jax.random.key(seed), 9)
    return {
        "query_raw": centred(arg_keys[0], (TOKENS, CH), 1.0, 6.0, ((0, 16), (1, 2))),
        "key_raw": centred(arg_keys[1], (TOKENS, CH), 1.0, 6.0, ((0, 16), (1, 2))),
        "value_raw": centred(arg_keys[2], (TOKENS, CH), 1.0, 6.0, ((0, 16), (1, 2))),
        "gate_raw": draw_gate_raw(jax.random.fold_in(arg_keys[8], 71), 0),
        "beta_raw": draw_beta_raw(jax.random.fold_in(arg_keys[8], 71), 0),
        "conv_weight": centred(arg_keys[5], (3, KCONV, CH), KCONV ** -0.5, 3.0, ((2, 2),), jnp.float32),
        "decay_log": draw_decay_log(jax.random.fold_in(arg_keys[8], 71), 0),
        "grad_out": centred(arg_keys[7], (TOKENS, CH), 1.0, 6.0, ((0, 16), (1, 2))),
    }


largest_entry = lax.Precision.HIGHEST
epsilon = 1e-06

def conv_silu(source, weights):
    margin = weights.shape[0] - 1
    length = source.shape[0]
    padded = jnp.concatenate([jnp.zeros((margin, source.shape[1]), jnp.float32), source], 0)
    summed = weights[0] * padded[0:length]
    for offset in range(1, weights.shape[0]):
        summed = summed + weights[offset] * padded[offset:offset + length]
    return jax.nn.silu(summed)

def unit_heads(vectors):
    return vectors * lax.rsqrt(lax.optimization_barrier(jnp.sum(vectors * vectors, axis=-1, keepdims=True)) + epsilon)

def layer_outputs(query_in, key_in, value_in, gate_in, beta_in, conv_in, decay_in):
    length = gate_in.shape[0]
    head_count = beta_in.shape[1]
    head_width = gate_in.shape[1] // head_count
    head_shape = (length, head_count, head_width)
    queries = unit_heads(conv_silu(query_in, conv_in[0]).reshape(head_shape))
    keys = unit_heads(conv_silu(key_in, conv_in[1]).reshape(head_shape))
    values = conv_silu(value_in, conv_in[2]).reshape(head_shape)
    log_decay = (-jnp.exp(decay_in) * jax.nn.softplus(gate_in)).reshape(head_shape)
    beta_rate = jax.nn.sigmoid(beta_in)
    block_count = length // TOK_DEV

    def token_step(recall_memory, sliced):
        single_query_row, single_key_row, value_row, decay_row, beta_row = sliced
        recall_memory = recall_memory * jnp.exp(decay_row)[:, :, None]
        predicted_value = jnp.einsum('pjf,pj->pf', recall_memory, single_key_row, precision=largest_entry)
        recall_memory = recall_memory + beta_row[:, None, None] * single_key_row[:, :, None] * (value_row - predicted_value)[:, None, :]
        return (recall_memory, jnp.einsum('pjf,pj->pf', recall_memory, single_query_row, precision=largest_entry))

    def block_step(recall_memory, sliced):
        return lax.scan(token_step, recall_memory, sliced)
    blocked = tuple((array.reshape((block_count, TOK_DEV) + array.shape[1:]) for array in (queries, keys, values, log_decay, beta_rate)))
    initial = jnp.zeros((head_count, head_width, head_width), jnp.float32)
    unused, outputs = lax.scan(jax.checkpoint(block_step), initial, blocked)
    return outputs.reshape(length, head_count * head_width)

def reference(query_raw, key_raw, value_raw, gate_raw, beta_raw, conv_weight, decay_log, grad_out):
    primal, pullback = jax.vjp(layer_outputs, query_raw.astype(jnp.float32), key_raw.astype(jnp.float32), value_raw.astype(jnp.float32), gate_raw, beta_raw, conv_weight, decay_log)
    grads = pullback(grad_out.astype(jnp.float32))
    return (grads[0].astype(jnp.bfloat16), grads[1].astype(jnp.bfloat16), grads[2].astype(jnp.bfloat16), grads[3], grads[4], grads[5], grads[6])
```

```python
import functools
import math

import jax
import jax.numpy as jnp
from jax import lax
from jax.experimental import pallas as pl
from jax.experimental.pallas import tpu as pltpu
from jax.sharding import PartitionSpec as P

F32 = jnp.float32
BF16 = jnp.bfloat16
EPS = 1e-06
PAD = 8
RED = 16
LAST = 16
GROUP = 2
TEAM = 8
VMEM_LIMIT = 64000000


def split(x):
    hi = x.astype(BF16)
    return hi, (x - hi.astype(F32)).astype(BF16)


def pack(x):
    return jnp.concatenate(split(x), 1)


def fold(out):
    n = out.shape[1] // 2
    return out[:, :n] + out[:, n:]


def dot(a, b, ta=False, tb=False):
    return lax.dot_general(
        a, b, (((0 if ta else 1,), (1 if tb else 0,)), ((), ())), preferred_element_type=F32
    )


def twice(x):
    return jnp.concatenate([x, x], 0)


def tall(x):
    n = x.shape[1] // 2
    return jnp.concatenate([x[:, :n], x[:, n:]], 0)


def cross_rows(x):
    n = x.shape[1] // 2
    hi, lo = x[:, :n], x[:, n:]
    return jnp.concatenate(
        [jnp.concatenate([hi, hi], 1), jnp.concatenate([lo, lo], 1)], 0
    )


def nn(a, b):
    return fold(dot(a, twice(b)))


def nt(a, b):
    return fold(dot(a, cross_rows(b), tb=True))


def tn(a, b):
    return fold(dot(tall(a), twice(b), ta=True))


def mm(a, b):
    return nn(pack(a), pack(b))


def ones_mm(ones, x, parts):
    rest, terms = x, []
    for _ in range(parts):
        term = rest.astype(BF16)
        terms.append(term)
        rest = rest - term.astype(F32)
    n = x.shape[1]
    out = jnp.dot(ones.astype(BF16), jnp.concatenate(terms, 1), preferred_element_type=F32)
    total = out[:, :n]
    for i in range(1, parts):
        total = total + out[:, i * n : (i + 1) * n]
    return total


def sigmoid(x):
    return 1.0 / (1.0 + jnp.exp(-x))


def softplus(x):
    return jnp.maximum(x, 0.0) + jnp.log1p(jnp.exp(-jnp.abs(x)))


def iotas(size):
    r = lax.broadcasted_iota(jnp.int32, (size, size), 0)
    c = lax.broadcasted_iota(jnp.int32, (size, size), 1)
    return r, c


def conv_pre(ext, x_ref, halo_ref, w_ref, j, cols):
    size = x_ref.shape[0]
    ext[0:PAD, :] = halo_ref[j, :, cols].astype(F32)
    ext[PAD : PAD + size, :] = x_ref[:, cols].astype(F32)
    taps = w_ref.shape[1]
    pre = None
    for i in range(taps):
        start = PAD - taps + 1 + i
        term = w_ref[j, i : i + 1, cols] * ext[start : start + size, :]
        pre = term if pre is None else pre + term
    return pre


def pick_column(ref, index):
    row = ref[pl.ds(index, 1), :]
    r, c = iotas(row.shape[1])
    return jnp.sum(jnp.where(r == c, row, 0.0), axis=1, keepdims=True)


def unit(x):
    r = lax.rsqrt(jnp.sum(x * x, axis=1, keepdims=True) + EPS)
    return x * r, r


def decays(gate, dlog):
    size = gate.shape[0]
    half = size // 2
    r, c = iotas(size)
    speed = -jnp.exp(dlog)
    ld = speed * softplus(gate)
    cum = ones_mm(jnp.where(r >= c, 1.0, 0.0), ld, 3)
    row = lax.broadcasted_iota(jnp.int32, gate.shape, 0)
    first = row < half
    mid = jnp.where(
        first, cum[half // 2 : half // 2 + 1, :], cum[half + half // 2 : half + half // 2 + 1, :]
    )
    edge = cum[half - 1 : half, :]
    last = cum[size - 1 : size, :]
    up = jnp.exp(cum - mid)
    down = jnp.exp(mid - cum)
    cross = jnp.exp(jnp.where(first, edge - cum, cum - edge))
    full = jnp.exp(cum)
    end = jnp.exp(last - cum)
    return ld, speed * sigmoid(gate), up, down, cross, full, end, jnp.exp(last)


def unit_inverses(coups):
    size = coups[0].shape[0]
    r, c = iotas(size)
    ident = jnp.where(r == c, 1.0, 0.0)
    shift = 3
    inside = (r >> shift) == (c >> shift)
    small = [jnp.where(inside, a, 0.0) for a in coups]
    p2 = [mm(a, a) for a in small]
    base = [ident - a for a in small]
    p4 = [mm(p, p) for p in p2]
    base = [x + mm(x, p) for x, p in zip(base, p2)]
    d = [x + mm(x, p) for x, p in zip(base, p4)]
    while (1 << shift) < size:
        joined = ((r >> (shift + 1)) == (c >> (shift + 1))) & ((r >> shift) != (c >> shift))
        low = [mm(jnp.where(joined, a, 0.0), x) for a, x in zip(coups, d)]
        d = [x - mm(x, y) for x, y in zip(d, low)]
        shift += 1
    return d


NAMES = (
    "q", "k", "v", "up", "down", "cross", "full", "end", "ld", "slope", "beta",
    "sq", "sk", "sv", "qr", "kr", "raw", "u", "reach",
)


def meet(start, step, count):
    if count & (count - 1):
        return lax.rem(start + step, count)
    out, bit = 0, 1
    while bit < count:
        out = out + lax.rem(start // bit + step // bit, 2) * bit
        bit *= 2
    return out


def layer_kernel(
    group,
    q_hbm, k_hbm, v_hbm, gate_hbm, beta_hbm, w_hbm, dlog_hbm, grad_hbm,
    dq_ref, dk_ref, dv_ref, dgate_ref, dbeta_ref, conv_ref, decay_ref,
    q_ref, k_ref, v_ref, gate_ref, beta_ref, w_ref, dlog_ref, grad_ref, load,
    keep, wk, ki, kd, kc, ups, crs, inv_sp, ke_sp, dend_row,
    ext, dext, halo_in,
    map_out, off_out, map_in, off_in, out_s, out_g, state_in, cotan_in,
    in_s, in_g, send_s, send_g,
    red_level, red_team, tail_out, tail_in, last_rows,
    hs, hr, ms, mr, fs, fr, ss, sr, gs, gr, cs, cr, ds, dr, ts, tr, ls, lr, es, er,
):
    n = lax.axis_size("seq")
    me = lax.axis_index("seq")
    team, part = map_in.shape[0], map_in.shape[1]
    mine = lax.rem(me, team)
    base = me - mine
    level = me // team
    levels = n // team
    mesh_id = pl.DeviceIdType.MESH
    right = lax.rem(me + 1, n)
    left = lax.rem(me + n - 1, n)
    size = q_ref.shape[0]
    half = size // 2
    heads, width = map_out.shape[0], map_out.shape[2]
    blocks = heads // group
    own_block = (mine * part) // group

    loads = [
        pltpu.make_async_copy(src, dst, load.at[i])
        for i, (src, dst) in enumerate((
            (q_hbm, q_ref), (k_hbm, k_ref), (v_hbm, v_ref), (gate_hbm, gate_ref),
            (dlog_hbm, dlog_ref), (w_hbm, w_ref), (beta_hbm, beta_ref), (grad_hbm, grad_ref),
        ))
    ]
    for copy in loads:
        copy.start()
    barrier = pltpu.get_barrier_semaphore()
    links = [base + lax.rem(mine + i, team) for i in range(1, team)]
    links += [lax.rem(me + i * team, n) for i in range(1, levels)]
    links += [right, left]
    for peer in links:
        pl.semaphore_signal(barrier, inc=1, device_id={"seq": peer}, device_id_type=mesh_id)
    for copy in loads:
        copy.wait()
    pl.semaphore_wait(barrier, len(links))

    def remote(src, dst, send, recv, to):
        return pltpu.make_async_remote_copy(
            src_ref=src, dst_ref=dst, send_sem=send, recv_sem=recv,
            device_id={"seq": to}, device_id_type=mesh_id,
        )

    def halo_copy(j, ref):
        return remote(
            ref.at[pl.ds(size - PAD, PAD)], halo_in.at[j], hs.at[j], hr.at[j], right
        )

    raws = (q_ref, k_ref, v_ref)

    @pl.when(me < n - 1)
    def _():
        for j, ref in enumerate(raws):
            halo_copy(j, ref).start()

    def block(member):
        return pl.ds(member * part, part)

    def lanes(head):
        return pl.ds(pl.multiple_of(head * width, width), width)

    def map_copy(source, target):
        return remote(
            map_out.at[block(target)], map_in.at[source], ms.at[target], mr.at[source],
            base + target,
        )

    def off_copy(source, target):
        return remote(
            off_out.at[block(target)], off_in.at[source], fs.at[target], fr.at[source],
            base + target,
        )

    def state_give(owner, member):
        return remote(
            out_s.at[member], state_in.at[block(owner)], ss.at[member], sr.at[owner],
            base + member,
        )

    def cotan_give(owner, member):
        return remote(
            out_g.at[member], cotan_in.at[block(owner)], gs.at[member], gr.at[owner],
            base + member,
        )

    state_hop = remote(send_s, in_s, cs, cr, lax.rem(me + team, n))
    cotan_hop = remote(send_g, in_g, ds, dr, lax.rem(me + n - team, n))

    def saved(head):
        spot = keep.at[head]
        return {name: spot.at[i] for i, name in enumerate(NAMES)}

    r, c = iotas(size)
    rr, cc = iotas(width)
    low = c < half

    @pl.when(me == 0)
    def _():
        halo_in[...] = jnp.zeros_like(halo_in)

    @pl.when(me > 0)
    def _():
        for j, ref in enumerate(raws):
            halo_copy(j, ref).wait_recv()

    def maps(step):
        start = meet(own_block, blocks - 1 - step, blocks) * group
        held = []
        for g in range(group):
            head = start + g
            cols = lanes(head)
            s = saved(head)
            ld, slope, up, down, cross, full, end, dend = decays(
                gate_ref[:, cols], dlog_ref[:, cols]
            )
            acts = []
            for j, ref in enumerate(raws):
                pre = conv_pre(ext.at[head * 3 + j], ref, halo_in, w_ref, j, cols)
                sig = sigmoid(pre)
                s[("sq", "sk", "sv")[j]][...] = sig * (1.0 + pre * (1.0 - sig))
                acts.append(pre * sig)
            q, qr = unit(acts[0])
            k, kr = unit(acts[1])
            v = acts[2]
            beta = jnp.broadcast_to(sigmoid(pick_column(beta_ref, head)), (size, width))
            for name, value in (
                ("q", q), ("k", k), ("v", v), ("up", up), ("down", down), ("cross", cross),
                ("full", full), ("end", end), ("ld", ld), ("slope", slope), ("beta", beta),
                ("qr", jnp.broadcast_to(qr, (size, width))),
                ("kr", jnp.broadcast_to(kr, (size, width))),
            ):
                s[name][...] = value
            dend_row[head] = jnp.broadcast_to(dend, (8, width))
            kfull = k * full
            ups_sp = pack(jnp.concatenate([q * up, k * up], 0))
            ups[head] = ups_sp
            kd_sp = pack(k * down)
            kd[head] = kd_sp
            kcross = k * cross
            kc_sp = pack(kcross)
            kc[head] = kc_sp
            crs_sp = pack(jnp.concatenate([(q * cross)[half:], kcross[half:]], 0))
            crs[head] = crs_sp
            same = nt(ups_sp, kd_sp)
            other = nt(crs_sp, kc_sp)
            rest = size - half
            att = jnp.concatenate(
                [same[:half], jnp.where(low[half:], other[:rest], same[half:size])], 0
            )
            raw = jnp.concatenate(
                [same[size : size + half], jnp.where(low[half:], other[rest:], same[size + half :])],
                0,
            )
            att = jnp.where(r >= c, att, 0.0)
            raw = jnp.where(r > c, raw, 0.0)
            s["raw"][...] = raw
            grad = grad_ref[:, cols]
            ah, al = split(att)
            both = dot(jnp.concatenate([ah, al], 1), grad, ta=True)
            reach = both[:size] + both[size:]
            s["reach"][...] = reach
            wk[head, size:, :] = pack(kfull)
            ke_sp[head] = pack(k * end)
            held.append((raw * beta, beta * kfull, beta * v, pack(q * full), reach, dend))
        invs = unit_inverses([item[0] for item in held])
        for g in range(group):
            head = start + g
            cols = lanes(head)
            s = saved(head)
            isp = pack(invs[g])
            inv_sp[head] = isp
            by = nn(isp, pack2(held[g][1], held[g][2]))
            s["u"][...] = by[:, width:]
            bh, bl = split(by)
            wsp = jnp.concatenate([bh[:, :width], bl[:, :width]], 1)
            wk[head, :size, :] = wsp
            ends = tn(ke_sp[head], jnp.concatenate([bh, bl], 1))
            full_map = jnp.where(rr == cc, held[g][5], 0.0) - ends[:, :width]
            map_hi = full_map.astype(BF16)
            left_over = jnp.sum(
                jnp.where(rr == cc, full_map - map_hi.astype(F32), 0.0), axis=0, keepdims=True
            )
            map_out[head, :width, :] = map_hi
            map_out[head, width:, :] = jnp.broadcast_to(left_over, (16, width)).astype(BF16)
            off_out[head, :width, :] = ends[:, width:]
            grad = grad_ref[:, cols]
            gsp = jnp.concatenate([grad, jnp.zeros_like(grad)], 1)
            off_out[head, width:, :] = tn(
                jnp.concatenate([held[g][3], -wsp], 0),
                jnp.concatenate([gsp, pack(held[g][4])], 0),
            )
        for g in range(group):
            head = start + g
            target = head // part

            @pl.when((target != mine) & (lax.rem(head, part) == part - 1))
            def _():
                map_copy(mine, target).start()
                off_copy(mine, target).start()

    for step in range(blocks):
        maps(step)
    map_in[mine] = map_out[block(mine)]
    off_in[mine] = off_out[block(mine)]

    def step_maps(j, h):
        both = map_in[j, h]
        rest = jnp.where(rr == cc, both[width : width + 1, :].astype(F32), 0.0).astype(BF16)
        return both[:width], rest

    def forward_step(j, h, state):
        hi, rest = step_maps(j, h)
        return nn(jnp.concatenate([hi, rest], 1), pack(state)) + off_in[j, h, :width, :]

    def backward_step(j, h, cotan):
        hi, rest = step_maps(j, h)
        out = fold(dot(jnp.concatenate([hi, rest], 0), twice(pack(cotan)), ta=True))
        return out + off_in[j, h, width:, :]

    def arrive(j):
        @pl.when(j != mine)
        def _():
            map_copy(j, j).wait_recv()
            off_copy(j, j).wait_recv()

    def forward(first):
        @pl.when(level == 0)
        def _():
            in_s[...] = jnp.zeros_like(in_s)

        @pl.when(level > 0)
        def _():
            state_hop.wait_recv()

        states = [in_s[h] for h in range(part)]
        for j in range(team):
            if first:
                arrive(j)
            for h in range(part):
                out_s[j, h] = states[h]
                states[h] = forward_step(j, h, states[h])

        @pl.when(level < levels - 1)
        def _():
            for h in range(part):
                send_s[h] = states[h]
            state_hop.start()

        state_in[block(mine)] = out_s[mine]
        for i in range(1, team):
            state_give(mine, meet(mine, i, team)).start()

    def backward(first):
        @pl.when(level == levels - 1)
        def _():
            in_g[...] = jnp.zeros_like(in_g)

        @pl.when(level < levels - 1)
        def _():
            cotan_hop.wait_recv()

        cotans = [in_g[h] for h in range(part)]
        for j in range(team - 1, -1, -1):
            if first:
                arrive(j)
            for h in range(part):
                out_g[j, h] = cotans[h]
                cotans[h] = backward_step(j, h, cotans[h])

        @pl.when(level > 0)
        def _():
            for h in range(part):
                send_g[h] = cotans[h]
            cotan_hop.start()

        cotan_in[block(mine)] = out_g[mine]
        for i in range(1, team):
            cotan_give(mine, meet(mine, i, team)).start()

    def ready(head):
        s = saved(head)
        isp = inv_sp[head]
        rh, rl = split(s["reach"][...])
        esp = ke_sp[head]
        rhs = jnp.concatenate([rh, esp[:, :width], rl, esp[:, width:]], 1)
        out = tn(isp, rhs)
        s["reach"][...] = out[:, :width]
        ki[head] = pack(out[:, width:])

    for head in range(heads // 2):
        ready(head)

    @pl.when(level < levels // 2)
    def _():
        forward(True)

    @pl.when(level >= levels // 2)
    def _():
        backward(True)

    for head in range(heads // 2, heads):
        ready(head)

    @pl.when(level < levels // 2)
    def _():
        backward(False)

    @pl.when(level >= levels // 2)
    def _():
        forward(False)

    def level_copy(b, source, target):
        spot = red_level.at[source, pl.ds(b * group, group)]
        return remote(
            spot, spot, ts.at[target, b], tr.at[source, b], lax.rem(target * team + mine, n)
        )

    def team_copy(b, source, target):
        spot = red_team.at[source, pl.ds(b * group, group)]
        return remote(spot, spot, ls.at[target, b], lr.at[source, b], base + target)

    def tail_copy(b):
        spot = pl.ds(b * group, group)
        return remote(tail_out.at[spot], tail_in.at[spot], es.at[b], er.at[b], left)

    other_levels = [lax.rem(level + i, levels) for i in range(1, levels)]
    others = [meet(mine, i, team) for i in range(1, team)]
    upper = jnp.where(c >= r, 1.0, 0.0)
    ones8 = jnp.ones((8, width), BF16)
    taps = w_ref.shape[1]

    def grads(b):
        for g in range(group):
            head = b * group + g
            owner = head // part

            @pl.when((owner != mine) & (lax.rem(head, part) == 0))
            def _():
                state_give(owner, owner).wait_recv()
                cotan_give(owner, owner).wait_recv()

        for g in range(group):
            head = b * group + g
            cols = lanes(head)
            s = saved(head)
            state, cotan = state_in[head], cotan_in[head]
            ssp, csp = pack(state), pack(cotan)
            wkx = nn(wk[head], ssp)
            deltas = s["u"][...] - wkx[:size]
            resid = s["v"][...] - wkx[size:]
            d_err = s["reach"][...] + nn(ki[head], csp)
            beta = s["beta"][...]
            d_v = beta * d_err
            grad = grad_ref[:, cols]
            esp = pack(d_err)
            lhs = jnp.concatenate(
                [jnp.concatenate([grad, jnp.zeros_like(grad)], 1), esp], 0
            )
            dsp = pack(deltas)
            to_full = nt(lhs, ssp)
            scores = nt(lhs, dsp)
            d_ke = nt(dsp, csp)
            d_att = jnp.where(r >= c, scores[:size], 0.0)
            d_coup = jnp.where(r > c, -scores[size:], 0.0)
            d_beta = jnp.sum(
                d_err * resid + d_coup * s["raw"][...], axis=1, keepdims=True
            )
            d_raw = d_coup * beta
            crossed = jnp.concatenate(
                [jnp.where(low[half:], d_att[half:], 0.0), jnp.where(low[half:], d_raw[half:], 0.0)],
                0,
            )
            both = jnp.concatenate(
                [
                    d_att[:half], jnp.where(low[half:], 0.0, d_att[half:]),
                    d_raw[:half], jnp.where(low[half:], 0.0, d_raw[half:]),
                ],
                0,
            )
            bsp, xsp = pack(both), pack(crossed)
            from_same = nn(bsp, kd[head])
            from_other = nn(xsp, kc[head])
            to_down = tn(bsp, ups[head])
            to_cross = tn(xsp, crs[head])
            up, cross, full, end = s["up"][...], s["cross"][...], s["full"][...], s["end"][...]
            q, k = s["q"][...], s["k"][...]
            rest = size - half
            d_q = from_same[:size] * up + to_full[:size] * full
            d_q = jnp.concatenate([d_q[:half], d_q[half:] + from_other[:rest] * cross[half:]], 0)
            d_k_up = from_same[size:] * up - (beta * to_full[size:]) * full
            d_k_up = jnp.concatenate(
                [d_k_up[:half], d_k_up[half:] + from_other[rest:] * cross[half:]], 0
            )
            k_end_part = d_ke * end
            d_k_down = to_down * s["down"][...] + k_end_part
            d_k_down = jnp.concatenate(
                [d_k_down[:half] + to_cross[:half] * cross[:half], d_k_down[half:]], 0
            )
            d_k = d_k_up + d_k_down
            d_cum = q * d_q + k * (d_k_up - d_k_down)
            end_state = fold(dot(ones8, tall(pack(state * cotan)), tb=True))[0:1, :]
            d_last = (
                jnp.sum(k * k_end_part, axis=0, keepdims=True)
                + dend_row[head, 0:1, :] * end_state
            )
            d_ld = ones_mm(upper, d_cum, 2) + d_last
            dgate_ref[:, cols] = s["slope"][...] * d_ld
            d_dlog = jnp.sum(s["ld"][...] * d_ld, axis=0, keepdims=True)
            d_braw = d_beta * (beta * (1.0 - beta))
            dbeta_ref[pl.ds(head, 1), :] = jnp.sum(
                jnp.where(r == c, d_braw, 0.0), axis=0, keepdims=True
            )
            d_q = s["qr"][...] * (d_q - q * jnp.sum(q * d_q, axis=1, keepdims=True))
            d_k = s["kr"][...] * (d_k - k * jnp.sum(k * d_k, axis=1, keepdims=True))
            red = []
            for j, (d_act, slope, out_ref) in enumerate(
                ((d_q, "sq", dq_ref), (d_k, "sk", dk_ref), (d_v, "sv", dv_ref))
            ):
                d_pre = d_act * s[slope][...]
                spot = dext.at[3 * g + j]
                spot[0:PAD, :] = jnp.zeros((PAD, width), F32)
                spot[PAD : PAD + size, :] = d_pre
                spot[PAD + size :, :] = jnp.zeros((PAD, width), F32)
                whole, tail = None, None
                for i in range(taps):
                    w = w_ref[j, i : i + 1, cols]
                    start = PAD + taps - 1 - i
                    term = w * spot[start : start + size, :]
                    edge = w * spot[taps - 1 - i : taps - 1 - i + PAD, :]
                    whole = term if whole is None else whole + term
                    tail = edge if tail is None else tail + edge
                    begin = PAD - taps + 1 + i
                    x = ext[head * 3 + j, begin : begin + size, :]
                    red.append(jnp.sum(d_pre * x, axis=0, keepdims=True))
                out_ref[:, cols] = whole.astype(BF16)
                tail_out[head, j * PAD : (j + 1) * PAD, :] = tail
                last_rows[head, j * LAST : (j + 1) * LAST, :] = whole[size - LAST :, :]
            red.append(d_dlog)
            red.append(jnp.zeros((RED - len(red), width), F32))
            red_level[level, head] = jnp.concatenate(red, 0)
        for other in other_levels:
            level_copy(b, level, other).start()

        @pl.when(me > 0)
        def _():
            tail_copy(b).start()

    def sum_levels(b):
        for other in other_levels:
            level_copy(b, other, other).wait_recv()
        spot = pl.ds(b * group, group)
        total = red_level[0, spot]
        for i in range(1, levels):
            total = total + red_level[i, spot]
        red_team[mine, spot] = total
        for other in others:
            team_copy(b, mine, other).start()

    order = [meet(own_block, i, blocks) for i in range(blocks)]
    for i in range(blocks):
        grads(order[i])
        if i:
            sum_levels(order[i - 1])
    sum_levels(order[-1])

    @pl.when(me == n - 1)
    def _():
        tail_in[...] = jnp.zeros_like(tail_in)

    for b in order:
        @pl.when(me < n - 1)
        def _():
            tail_copy(b).wait_recv()

    for head in range(heads):
        cols = slice(head * width, (head + 1) * width)
        for j, out_ref in enumerate((dq_ref, dk_ref, dv_ref)):
            rows = last_rows[head, j * LAST : (j + 1) * LAST, :]
            rows = jnp.concatenate(
                [rows[: LAST - PAD], rows[LAST - PAD :] + tail_in[head, j * PAD : (j + 1) * PAD, :]],
                0,
            )
            out_ref[size - LAST :, cols] = rows.astype(BF16)

    for b in order:
        for other in others:
            team_copy(b, other, other).wait_recv()
    for head in range(heads):
        cols = slice(head * width, (head + 1) * width)
        total = red_team[0, head]
        for i in range(1, team):
            total = total + red_team[i, head]
        for j in range(3):
            conv_ref[j, :, cols] = total[j * taps : (j + 1) * taps, :]
        decay_ref[:, cols] = total[3 * taps : 3 * taps + 1, :]

    for other in others:
        map_copy(mine, other).wait_send()
        off_copy(mine, other).wait_send()
        state_give(mine, other).wait_send()
        cotan_give(mine, other).wait_send()
        for b in order:
            team_copy(b, mine, other).wait_send()
    for other in other_levels:
        for b in order:
            level_copy(b, level, other).wait_send()

    @pl.when(me > 0)
    def _():
        for b in order:
            tail_copy(b).wait_send()

    @pl.when(level < levels - 1)
    def _():
        state_hop.wait_send()

    @pl.when(level > 0)
    def _():
        cotan_hop.wait_send()

    @pl.when(me < n - 1)
    def _():
        for j, ref in enumerate(raws):
            halo_copy(j, ref).wait_send()


def pack2(a, b):
    ah, al = split(a)
    bh, bl = split(b)
    return jnp.concatenate([ah, bh, al, bl], 1)


def write_kernel(count, *refs):
    sources, targets, spots = refs[:count], refs[count : 2 * count], refs[2 * count : 3 * count]
    sems = refs[-1]
    reads = [
        pltpu.make_async_copy(src, spot, sems.at[0, i])
        for i, (src, spot) in enumerate(zip(sources, spots))
    ]
    writes = [
        pltpu.make_async_copy(spot, dst, sems.at[1, i])
        for i, (spot, dst) in enumerate(zip(spots, targets))
    ]
    for copy in reads:
        copy.start()
    for i in range(count):
        reads[i].wait()
        writes[i].start()
    for copy in writes:
        copy.wait()


def per_device(query_raw, key_raw, value_raw, gate_raw, beta_raw, conv_weight, decay_log, grad_out):
    n = lax.axis_size("seq")
    size, channels = gate_raw.shape
    heads = beta_raw.shape[1]
    width = channels // heads
    group = GROUP if heads % GROUP == 0 else 1
    team = math.gcd(TEAM, math.gcd(n, heads))
    part = heads // team
    levels = n // team
    nblk = heads // group
    vmem = pl.BlockSpec(memory_space=pltpu.VMEM)
    hbm = pl.BlockSpec(memory_space=pltpu.HBM)
    act = jax.ShapeDtypeStruct((size, channels), BF16)
    shapes = (
        act, act, act,
        jax.ShapeDtypeStruct((size, channels), F32),
        jax.ShapeDtypeStruct((heads, size), F32),
        jax.ShapeDtypeStruct(conv_weight.shape, F32),
        jax.ShapeDtypeStruct((1, channels), F32),
    )

    def f32s(*shape):
        return pltpu.VMEM(shape, F32)

    def bf16s(*shape):
        return pltpu.VMEM(shape, BF16)

    def sems(*shape):
        return pltpu.SemaphoreType.DMA(shape)

    scratch = [
        pltpu.VMEM(query_raw.shape, query_raw.dtype), pltpu.VMEM(key_raw.shape, key_raw.dtype),
        pltpu.VMEM(value_raw.shape, value_raw.dtype), pltpu.VMEM(gate_raw.shape, F32),
        f32s(heads, size), pltpu.VMEM(conv_weight.shape, F32), f32s(1, channels),
        pltpu.VMEM(grad_out.shape, grad_out.dtype), sems(8),
        f32s(heads, len(NAMES), size, width),
        bf16s(heads, 2 * size, 2 * width), bf16s(heads, size, 2 * width),
        bf16s(heads, size, 2 * width), bf16s(heads, size, 2 * width),
        bf16s(heads, 2 * size, 2 * width), bf16s(heads, size, 2 * width),
        bf16s(heads, size, 2 * size), bf16s(heads, size, 2 * width),
        f32s(heads, 8, width),
        f32s(3 * heads, PAD + size, width), f32s(3 * group, PAD + size + PAD, width),
        pltpu.VMEM((3, PAD, channels), query_raw.dtype),
        bf16s(heads, width + 16, width), f32s(heads, 2 * width, width),
        bf16s(team, part, width + 16, width), f32s(team, part, 2 * width, width),
        f32s(team, part, width, width), f32s(team, part, width, width),
        f32s(heads, width, width), f32s(heads, width, width),
        f32s(part, width, width), f32s(part, width, width),
        f32s(part, width, width), f32s(part, width, width),
        f32s(levels, heads, RED, width), f32s(team, heads, RED, width),
        f32s(heads, 3 * PAD, width), f32s(heads, 3 * PAD, width),
        f32s(heads, 3 * LAST, width),
        sems(3), sems(3),
        sems(team), sems(team), sems(team), sems(team),
        sems(team), sems(team), sems(team), sems(team),
        pltpu.SemaphoreType.DMA, pltpu.SemaphoreType.DMA,
        pltpu.SemaphoreType.DMA, pltpu.SemaphoreType.DMA,
        sems(levels, nblk), sems(levels, nblk), sems(team, nblk), sems(team, nblk),
        sems(nblk), sems(nblk),
    ]
    results = pl.pallas_call(
        functools.partial(layer_kernel, group),
        out_shape=shapes,
        in_specs=[hbm] * 8,
        out_specs=(vmem,) * 7,
        scratch_shapes=scratch,
        compiler_params=pltpu.CompilerParams(
            collective_id=0, has_side_effects=True, vmem_limit_bytes=VMEM_LIMIT
        ),
        name="layer",
    )(
        query_raw, key_raw, value_raw, gate_raw, beta_raw.T, conv_weight,
        decay_log.reshape(1, channels), grad_out,
    )
    dq, dk, dv, dgate, dbeta, conv_sum, decay_sum = pl.pallas_call(
        functools.partial(write_kernel, len(shapes)),
        out_shape=shapes,
        in_specs=[hbm] * 7,
        out_specs=(hbm,) * 7,
        scratch_shapes=[pltpu.VMEM(x.shape, x.dtype) for x in shapes] + [sems(2, 7)],
        compiler_params=pltpu.CompilerParams(vmem_limit_bytes=VMEM_LIMIT),
        name="write",
    )(*results)
    return (dq, dk, dv, dgate, dbeta.T, conv_sum, decay_sum.reshape(channels))


def solution(mesh):
    in_specs = (
        P("seq", "head"),
        P("seq", "head"),
        P("seq", "head"),
        P("seq", "head"),
        P("seq", "head"),
        P(None, None, "head"),
        P("head"),
        P("seq", "head"),
    )
    out_specs = (
        P("seq", "head"),
        P("seq", "head"),
        P("seq", "head"),
        P("seq", "head"),
        P("seq", "head"),
        P(None, None, "head"),
        P("head"),
    )
    return jax.shard_map(
        per_device, mesh=mesh, in_specs=in_specs, out_specs=out_specs, check_vma=False
    )
```

```python
import functools
import math

import jax
import jax.numpy as jnp
from jax import lax
from jax.experimental import pallas as pl
from jax.experimental.pallas import tpu as pltpu
from jax.sharding import PartitionSpec as P

F32 = jnp.float32
BF16 = jnp.bfloat16
EPS = 1e-06
PAD = 8
RED = 16
LAST = 16
GROUP = 2
TEAM = 8
VMEM_LIMIT = 64000000


def split(x):
    hi = x.astype(BF16)
    return hi, (x - hi.astype(F32)).astype(BF16)


def pack(x):
    return jnp.concatenate(split(x), 1)


def fold(out):
    n = out.shape[1] // 2
    return out[:, :n] + out[:, n:]


def dot(a, b, ta=False, tb=False):
    return lax.dot_general(
        a, b, (((0 if ta else 1,), (1 if tb else 0,)), ((), ())), preferred_element_type=F32
    )


def twice(x):
    return jnp.concatenate([x, x], 0)


def tall(x):
    n = x.shape[1] // 2
    return jnp.concatenate([x[:, :n], x[:, n:]], 0)


def cross_rows(x):
    n = x.shape[1] // 2
    hi, lo = x[:, :n], x[:, n:]
    return jnp.concatenate(
        [jnp.concatenate([hi, hi], 1), jnp.concatenate([lo, lo], 1)], 0
    )


def nn(a, b):
    return fold(dot(a, twice(b)))


def nt(a, b):
    return fold(dot(a, cross_rows(b), tb=True))


def tn(a, b):
    return fold(dot(tall(a), twice(b), ta=True))


def mm(a, b):
    return nn(pack(a), pack(b))


def ones_mm(ones, x, parts):
    rest, terms = x, []
    for _ in range(parts):
        term = rest.astype(BF16)
        terms.append(term)
        rest = rest - term.astype(F32)
    n = x.shape[1]
    out = jnp.dot(ones.astype(BF16), jnp.concatenate(terms, 1), preferred_element_type=F32)
    total = out[:, :n]
    for i in range(1, parts):
        total = total + out[:, i * n : (i + 1) * n]
    return total


def sigmoid(x):
    return 1.0 / (1.0 + jnp.exp(-x))


def softplus(x):
    return jnp.maximum(x, 0.0) + jnp.log1p(jnp.exp(-jnp.abs(x)))


def iotas(size):
    r = lax.broadcasted_iota(jnp.int32, (size, size), 0)
    c = lax.broadcasted_iota(jnp.int32, (size, size), 1)
    return r, c


def conv_pre(ext, x_ref, halo_ref, w_ref, j, cols):
    size = x_ref.shape[0]
    ext[0:PAD, :] = halo_ref[j, :, cols].astype(F32)
    ext[PAD : PAD + size, :] = x_ref[:, cols].astype(F32)
    taps = w_ref.shape[1]
    pre = None
    for i in range(taps):
        start = PAD - taps + 1 + i
        term = w_ref[j, i : i + 1, cols] * ext[start : start + size, :]
        pre = term if pre is None else pre + term
    return pre


def pick_column(ref, index):
    row = ref[pl.ds(index, 1), :]
    r, c = iotas(row.shape[1])
    return jnp.sum(jnp.where(r == c, row, 0.0), axis=1, keepdims=True)


def unit(x):
    r = lax.rsqrt(jnp.sum(x * x, axis=1, keepdims=True) + EPS)
    return x * r, r


def decays(gate, dlog):
    size = gate.shape[0]
    half = size // 2
    r, c = iotas(size)
    speed = -jnp.exp(dlog)
    ld = speed * softplus(gate)
    cum = ones_mm(jnp.where(r >= c, 1.0, 0.0), ld, 3)
    row = lax.broadcasted_iota(jnp.int32, gate.shape, 0)
    first = row < half
    mid = jnp.where(
        first, cum[half // 2 : half // 2 + 1, :], cum[half + half // 2 : half + half // 2 + 1, :]
    )
    edge = cum[half - 1 : half, :]
    last = cum[size - 1 : size, :]
    up = jnp.exp(cum - mid)
    down = jnp.exp(mid - cum)
    cross = jnp.exp(jnp.where(first, edge - cum, cum - edge))
    full = jnp.exp(cum)
    end = jnp.exp(last - cum)
    return ld, speed * sigmoid(gate), up, down, cross, full, end, jnp.exp(last)


def unit_inverses(coups):
    size = coups[0].shape[0]
    r, c = iotas(size)
    ident = jnp.where(r == c, 1.0, 0.0)
    shift = 3
    inside = (r >> shift) == (c >> shift)
    small = [jnp.where(inside, a, 0.0) for a in coups]
    p2 = [mm(a, a) for a in small]
    base = [ident - a for a in small]
    p4 = [mm(p, p) for p in p2]
    base = [x + mm(x, p) for x, p in zip(base, p2)]
    d = [x + mm(x, p) for x, p in zip(base, p4)]
    while (1 << shift) < size:
        joined = ((r >> (shift + 1)) == (c >> (shift + 1))) & ((r >> shift) != (c >> shift))
        low = [mm(jnp.where(joined, a, 0.0), x) for a, x in zip(coups, d)]
        d = [x - mm(x, y) for x, y in zip(d, low)]
        shift += 1
    return d


NAMES = (
    "q", "k", "v", "up", "down", "cross", "full", "end", "ld", "slope", "beta",
    "sq", "sk", "sv", "qr", "kr", "raw", "u", "reach",
)


def meet(start, step, count):
    if count & (count - 1):
        return lax.rem(start + step, count)
    out, bit = 0, 1
    while bit < count:
        out = out + lax.rem(start // bit + step // bit, 2) * bit
        bit *= 2
    return out


def layer_kernel(
    group,
    q_hbm, k_hbm, v_hbm, gate_hbm, beta_hbm, w_hbm, dlog_hbm, grad_hbm,
    dq_out, dk_out, dv_out, dgate_out, dbeta_out, conv_ref, decay_ref,
    dq_ref, dk_ref, dv_ref, dgate_ref, dbeta_ref, store,
    q_ref, k_ref, v_ref, gate_ref, beta_ref, w_ref, dlog_ref, grad_ref, load,
    keep, wk, ki, kd, kc, ups, crs, inv_sp, ke_sp, dend_row,
    ext, dext, halo_in,
    map_out, off_out, map_in, off_in, out_s, out_g, state_in, cotan_in,
    in_s, in_g, send_s, send_g,
    red_level, red_team, tail_out, tail_in, last_rows,
    hs, hr, ms, mr, fs, fr, ss, sr, gs, gr, cs, cr, ds, dr, ts, tr, ls, lr, es, er,
):
    n = lax.axis_size("seq")
    me = lax.axis_index("seq")
    team, part = map_in.shape[0], map_in.shape[1]
    mine = lax.rem(me, team)
    base = me - mine
    level = me // team
    levels = n // team
    mesh_id = pl.DeviceIdType.MESH
    right = lax.rem(me + 1, n)
    left = lax.rem(me + n - 1, n)
    size = q_ref.shape[0]
    half = size // 2
    heads, width = map_out.shape[0], map_out.shape[2]
    blocks = heads // group
    own_block = (mine * part) // group

    loads = [
        pltpu.make_async_copy(src, dst, load.at[i])
        for i, (src, dst) in enumerate((
            (dlog_hbm, dlog_ref), (gate_hbm, gate_ref), (q_hbm, q_ref), (k_hbm, k_ref),
            (v_hbm, v_ref), (w_hbm, w_ref), (beta_hbm, beta_ref), (grad_hbm, grad_ref),
        ))
    ]
    for copy in loads:
        copy.start()
    barrier = pltpu.get_barrier_semaphore()
    links = [base + lax.rem(mine + i, team) for i in range(1, team)]
    links += [lax.rem(me + i * team, n) for i in range(1, levels)]
    links += [right, left]
    for peer in links:
        pl.semaphore_signal(barrier, inc=1, device_id={"seq": peer}, device_id_type=mesh_id)
    def remote(src, dst, send, recv, to):
        return pltpu.make_async_remote_copy(
            src_ref=src, dst_ref=dst, send_sem=send, recv_sem=recv,
            device_id={"seq": to}, device_id_type=mesh_id,
        )

    def halo_copy(j, ref):
        return remote(
            ref.at[pl.ds(size - PAD, PAD)], halo_in.at[j], hs.at[j], hr.at[j], right
        )

    raws = (q_ref, k_ref, v_ref)

    def block(member):
        return pl.ds(member * part, part)

    def lanes(head):
        return pl.ds(pl.multiple_of(head * width, width), width)

    def map_copy(source, target):
        return remote(
            map_out.at[block(target)], map_in.at[source], ms.at[target], mr.at[source],
            base + target,
        )

    def off_copy(slot, source, target):
        return remote(
            off_out.at[slot, block(target)], off_in.at[slot, source],
            fs.at[slot, target], fr.at[slot, source], base + target,
        )

    state_slot = 1
    if levels > 1:
        state_slot = level // (levels // 2)
        if levels % 2:
            state_slot = jnp.minimum(state_slot, 1)

    def state_give(owner, member):
        return remote(
            out_s.at[member], state_in.at[block(owner)], ss.at[member], sr.at[owner],
            base + member,
        )

    def cotan_give(owner, member):
        return remote(
            out_g.at[member], cotan_in.at[block(owner)], gs.at[member], gr.at[owner],
            base + member,
        )

    state_hop = remote(send_s, in_s, cs, cr, lax.rem(me + team, n))
    cotan_hop = remote(send_g, in_g, ds, dr, lax.rem(me + n - team, n))

    def saved(head):
        spot = keep.at[head]
        return {name: spot.at[i] for i, name in enumerate(NAMES)}

    r, c = iotas(size)
    rr, cc = iotas(width)
    low = c < half

    def block_at(step):
        return meet(own_block, blocks - 1 - step, blocks)

    def prepare(step):
        for g in range(group):
            slot = step * group + g
            cols = lanes(block_at(step) * group + g)
            s = saved(slot)
            parts = decays(gate_ref[:, cols], dlog_ref[:, cols])
            for name, value in zip(
                ("ld", "slope", "up", "down", "cross", "full", "end"), parts
            ):
                s[name][...] = value
            dend_row[slot] = jnp.broadcast_to(parts[-1], (8, width))

    loads[0].wait()
    loads[1].wait()
    for step in range(blocks // 2):
        prepare(step)
    for copy in loads[2:]:
        copy.wait()
    pl.semaphore_wait(barrier, len(links))

    @pl.when(me < n - 1)
    def _():
        for j, ref in enumerate(raws):
            halo_copy(j, ref).start()

    for step in range(blocks // 2, blocks):
        prepare(step)

    @pl.when(me == 0)
    def _():
        halo_in[...] = jnp.zeros_like(halo_in)

    @pl.when(me > 0)
    def _():
        for j, ref in enumerate(raws):
            halo_copy(j, ref).wait_recv()

    def front(step):
        start = block_at(step) * group
        held = []
        for g in range(group):
            head = start + g
            slot = step * group + g
            cols = lanes(head)
            s = saved(slot)
            up, down, cross = s["up"][...], s["down"][...], s["cross"][...]
            full, end = s["full"][...], s["end"][...]
            dend = dend_row[slot, 0:1, :]
            acts = []
            for j, ref in enumerate(raws):
                pre = conv_pre(ext.at[slot * 3 + j], ref, halo_in, w_ref, j, cols)
                sig = sigmoid(pre)
                s[("sq", "sk", "sv")[j]][...] = sig * (1.0 + pre * (1.0 - sig))
                acts.append(pre * sig)
            q, qr = unit(acts[0])
            k, kr = unit(acts[1])
            v = acts[2]
            beta = jnp.broadcast_to(sigmoid(pick_column(beta_ref, head)), (size, width))
            for name, value in (
                ("q", q), ("k", k), ("v", v), ("beta", beta),
                ("qr", jnp.broadcast_to(qr, (size, width))),
                ("kr", jnp.broadcast_to(kr, (size, width))),
            ):
                s[name][...] = value
            kfull = k * full
            ups_sp = pack(jnp.concatenate([q * up, k * up], 0))
            ups[slot] = ups_sp
            kd_sp = pack(k * down)
            kd[slot] = kd_sp
            kcross = k * cross
            kc_sp = pack(kcross)
            kc[slot] = kc_sp
            crs_sp = pack(jnp.concatenate([(q * cross)[half:], kcross[half:]], 0))
            crs[slot] = crs_sp
            same = nt(ups_sp, kd_sp)
            other = nt(crs_sp, kc_sp)
            rest = size - half
            att = jnp.concatenate(
                [same[:half], jnp.where(low[half:], other[:rest], same[half:size])], 0
            )
            raw = jnp.concatenate(
                [same[size : size + half], jnp.where(low[half:], other[rest:], same[size + half :])],
                0,
            )
            att = jnp.where(r >= c, att, 0.0)
            raw = jnp.where(r > c, raw, 0.0)
            s["raw"][...] = raw
            grad = grad_ref[:, cols]
            ah, al = split(att)
            both = dot(jnp.concatenate([ah, al], 1), grad, ta=True)
            reach = both[:size] + both[size:]
            s["reach"][...] = reach
            wk[slot, size:, :] = pack(kfull)
            ke_sp[slot] = pack(k * end)
            held.append((raw * beta, beta * kfull, beta * v, pack(q * full), reach, dend))
        return held

    def back(step, held, invs):
        start = block_at(step) * group
        for g in range(group):
            head = start + g
            slot = step * group + g
            cols = lanes(head)
            s = saved(slot)
            isp = pack(invs[g])
            inv_sp[slot] = isp
            by = nn(isp, pack2(held[g][1], held[g][2]))
            s["u"][...] = by[:, width:]
            bh, bl = split(by)
            wsp = jnp.concatenate([bh[:, :width], bl[:, :width]], 1)
            wk[slot, :size, :] = wsp
            ends = tn(ke_sp[slot], jnp.concatenate([bh, bl], 1))
            full_map = jnp.where(rr == cc, held[g][5], 0.0) - ends[:, :width]
            map_hi = full_map.astype(BF16)
            left_over = jnp.sum(
                jnp.where(rr == cc, full_map - map_hi.astype(F32), 0.0), axis=0, keepdims=True
            )
            map_out[head, :width, :] = map_hi
            map_out[head, width:, :] = jnp.broadcast_to(left_over, (16, width)).astype(BF16)
            off_out[state_slot, head] = ends[:, width:]
            grad = grad_ref[:, cols]
            gsp = jnp.concatenate([grad, jnp.zeros_like(grad)], 1)
            off_out[1 - state_slot, head] = tn(
                jnp.concatenate([held[g][3], -wsp], 0),
                jnp.concatenate([gsp, pack(held[g][4])], 0),
            )
        for g in range(group):
            head = start + g
            target = head // part

            @pl.when((target != mine) & (lax.rem(head, part) == part - 1))
            def _():
                map_copy(mine, target).start()
                off_copy(0, mine, target).start()

    def send_rest(step):
        start = block_at(step) * group
        for g in range(group):
            head = start + g
            target = head // part

            @pl.when((target != mine) & (lax.rem(head, part) == part - 1))
            def _():
                off_copy(1, mine, target).start()

    held = front(0)
    for step in range(blocks):
        invs = unit_inverses([item[0] for item in held])
        later = front(step + 1) if step + 1 < blocks else None
        back(step, held, invs)
        held = later
        if step:
            send_rest(step - 1)
    send_rest(blocks - 1)
    map_in[mine] = map_out[block(mine)]
    off_in[0, mine] = off_out[0, block(mine)]
    off_in[1, mine] = off_out[1, block(mine)]

    def step_maps(j, h):
        both = map_in[j, h]
        rest = jnp.where(rr == cc, both[width : width + 1, :].astype(F32), 0.0).astype(BF16)
        return both[:width], rest

    def forward_step(slot, j, h, state):
        hi, rest = step_maps(j, h)
        return nn(jnp.concatenate([hi, rest], 1), pack(state)) + off_in[slot, j, h]

    def backward_step(slot, j, h, cotan):
        hi, rest = step_maps(j, h)
        out = fold(dot(jnp.concatenate([hi, rest], 0), twice(pack(cotan)), ta=True))
        return out + off_in[slot, j, h]

    def arrive(slot, j):
        @pl.when(j != mine)
        def _():
            if slot == 0:
                map_copy(j, j).wait_recv()
            off_copy(slot, j, j).wait_recv()

    def forward(slot):
        @pl.when(level == 0)
        def _():
            in_s[...] = jnp.zeros_like(in_s)

        @pl.when(level > 0)
        def _():
            state_hop.wait_recv()

        states = [in_s[h] for h in range(part)]
        for j in range(team):
            arrive(slot, j)
            for h in range(part):
                out_s[j, h] = states[h]
                states[h] = forward_step(slot, j, h, states[h])

        @pl.when(level < levels - 1)
        def _():
            for h in range(part):
                send_s[h] = states[h]
            state_hop.start()

        state_in[block(mine)] = out_s[mine]
        for i in range(1, team):
            state_give(mine, meet(mine, i, team)).start()

    def backward(slot):
        @pl.when(level == levels - 1)
        def _():
            in_g[...] = jnp.zeros_like(in_g)

        @pl.when(level < levels - 1)
        def _():
            cotan_hop.wait_recv()

        cotans = [in_g[h] for h in range(part)]
        for j in range(team - 1, -1, -1):
            arrive(slot, j)
            for h in range(part):
                out_g[j, h] = cotans[h]
                cotans[h] = backward_step(slot, j, h, cotans[h])

        @pl.when(level > 0)
        def _():
            for h in range(part):
                send_g[h] = cotans[h]
            cotan_hop.start()

        cotan_in[block(mine)] = out_g[mine]
        for i in range(1, team):
            cotan_give(mine, meet(mine, i, team)).start()

    def ready(slot):
        s = saved(slot)
        isp = inv_sp[slot]
        rh, rl = split(s["reach"][...])
        esp = ke_sp[slot]
        rhs = jnp.concatenate([rh, esp[:, :width], rl, esp[:, width:]], 1)
        out = tn(isp, rhs)
        s["reach"][...] = out[:, :width]
        ki[slot] = pack(out[:, width:])

    @pl.when(level < levels // 2)
    def _():
        forward(0)

    @pl.when(level >= levels // 2)
    def _():
        backward(0)

    for slot in range(heads):
        ready(slot)

    @pl.when(level < levels // 2)
    def _():
        backward(1)

    @pl.when(level >= levels // 2)
    def _():
        forward(1)

    def level_copy(b, source, target):
        spot = red_level.at[source, pl.ds(b * group, group)]
        return remote(
            spot, spot, ts.at[target, b], tr.at[source, b], lax.rem(target * team + mine, n)
        )

    def team_copy(b, source, target):
        spot = red_team.at[source, pl.ds(b * group, group)]
        return remote(spot, spot, ls.at[target, b], lr.at[source, b], base + target)

    def tail_copy(b):
        spot = pl.ds(b * group, group)
        return remote(tail_out.at[spot], tail_in.at[spot], es.at[b], er.at[b], left)

    other_levels = [lax.rem(level + i, levels) for i in range(1, levels)]
    others = [meet(mine, i, team) for i in range(1, team)]
    upper = jnp.where(c >= r, 1.0, 0.0)
    ones8 = jnp.ones((8, width), BF16)
    taps = w_ref.shape[1]

    def grads(i):
        b = order[i]
        for g in range(group):
            head = b * group + g
            owner = head // part

            @pl.when((owner != mine) & (lax.rem(head, part) == 0))
            def _():
                state_give(owner, owner).wait_recv()
                cotan_give(owner, owner).wait_recv()

        for g in range(group):
            head = b * group + g
            slot = (blocks - 1 - i) * group + g
            cols = lanes(head)
            s = saved(slot)
            state, cotan = state_in[head], cotan_in[head]
            ssp, csp = pack(state), pack(cotan)
            wkx = nn(wk[slot], ssp)
            deltas = s["u"][...] - wkx[:size]
            resid = s["v"][...] - wkx[size:]
            d_err = s["reach"][...] + nn(ki[slot], csp)
            beta = s["beta"][...]
            d_v = beta * d_err
            grad = grad_ref[:, cols]
            esp = pack(d_err)
            lhs = jnp.concatenate(
                [jnp.concatenate([grad, jnp.zeros_like(grad)], 1), esp], 0
            )
            dsp = pack(deltas)
            to_full = nt(lhs, ssp)
            scores = nt(lhs, dsp)
            d_ke = nt(dsp, csp)
            d_att = jnp.where(r >= c, scores[:size], 0.0)
            d_coup = jnp.where(r > c, -scores[size:], 0.0)
            d_beta = jnp.sum(
                d_err * resid + d_coup * s["raw"][...], axis=1, keepdims=True
            )
            d_raw = d_coup * beta
            crossed = jnp.concatenate(
                [jnp.where(low[half:], d_att[half:], 0.0), jnp.where(low[half:], d_raw[half:], 0.0)],
                0,
            )
            both = jnp.concatenate(
                [
                    d_att[:half], jnp.where(low[half:], 0.0, d_att[half:]),
                    d_raw[:half], jnp.where(low[half:], 0.0, d_raw[half:]),
                ],
                0,
            )
            bsp, xsp = pack(both), pack(crossed)
            from_same = nn(bsp, kd[slot])
            from_other = nn(xsp, kc[slot])
            to_down = tn(bsp, ups[slot])
            to_cross = tn(xsp, crs[slot])
            up, cross, full, end = s["up"][...], s["cross"][...], s["full"][...], s["end"][...]
            q, k = s["q"][...], s["k"][...]
            rest = size - half
            d_q = from_same[:size] * up + to_full[:size] * full
            d_q = jnp.concatenate([d_q[:half], d_q[half:] + from_other[:rest] * cross[half:]], 0)
            d_k_up = from_same[size:] * up - (beta * to_full[size:]) * full
            d_k_up = jnp.concatenate(
                [d_k_up[:half], d_k_up[half:] + from_other[rest:] * cross[half:]], 0
            )
            k_end_part = d_ke * end
            d_k_down = to_down * s["down"][...] + k_end_part
            d_k_down = jnp.concatenate(
                [d_k_down[:half] + to_cross[:half] * cross[:half], d_k_down[half:]], 0
            )
            d_k = d_k_up + d_k_down
            d_cum = q * d_q + k * (d_k_up - d_k_down)
            end_state = fold(dot(ones8, tall(pack(state * cotan)), tb=True))[0:1, :]
            d_last = (
                jnp.sum(k * k_end_part, axis=0, keepdims=True)
                + dend_row[slot, 0:1, :] * end_state
            )
            d_ld = ones_mm(upper, d_cum, 2) + d_last
            dgate_ref[:, cols] = s["slope"][...] * d_ld
            d_dlog = jnp.sum(s["ld"][...] * d_ld, axis=0, keepdims=True)
            d_braw = d_beta * (beta * (1.0 - beta))
            dbeta_ref[pl.ds(head, 1), :] = jnp.sum(
                jnp.where(r == c, d_braw, 0.0), axis=0, keepdims=True
            )
            d_q = s["qr"][...] * (d_q - q * jnp.sum(q * d_q, axis=1, keepdims=True))
            d_k = s["kr"][...] * (d_k - k * jnp.sum(k * d_k, axis=1, keepdims=True))
            red = []
            for j, (d_act, slope) in enumerate(((d_q, "sq"), (d_k, "sk"), (d_v, "sv"))):
                d_pre = d_act * s[slope][...]
                spot = dext.at[3 * slot + j]
                spot[0:PAD, :] = jnp.zeros((PAD, width), F32)
                spot[PAD : PAD + size, :] = d_pre
                spot[PAD + size :, :] = jnp.zeros((PAD, width), F32)
                tail = None
                for tap in range(taps):
                    w = w_ref[j, tap : tap + 1, cols]
                    edge = w * spot[taps - 1 - tap : taps - 1 - tap + PAD, :]
                    tail = edge if tail is None else tail + edge
                    begin = PAD - taps + 1 + tap
                    x = ext[slot * 3 + j, begin : begin + size, :]
                    red.append(jnp.sum(d_pre * x, axis=0, keepdims=True))
                tail_out[head, j * PAD : (j + 1) * PAD, :] = tail
            red.append(d_dlog)
            red.append(jnp.zeros((RED - len(red), width), F32))
            red_level[level, head] = jnp.concatenate(red, 0)
        for other in other_levels:
            level_copy(b, level, other).start()

        @pl.when(me > 0)
        def _():
            tail_copy(b).start()

    def sum_levels(b):
        for other in other_levels:
            level_copy(b, other, other).wait_recv()
        spot = pl.ds(b * group, group)
        total = red_level[0, spot]
        for i in range(1, levels):
            total = total + red_level[i, spot]
        red_team[mine, spot] = total
        for other in others:
            team_copy(b, mine, other).start()

    def spread_back(i):
        for g in range(group):
            head = order[i] * group + g
            slot = (blocks - 1 - i) * group + g
            cols = lanes(head)
            for j, out_ref in enumerate((dq_ref, dk_ref, dv_ref)):
                spot = dext.at[3 * slot + j]
                whole = None
                for tap in range(taps):
                    start = PAD + taps - 1 - tap
                    term = w_ref[j, tap : tap + 1, cols] * spot[start : start + size, :]
                    whole = term if whole is None else whole + term
                out_ref[:, cols] = whole.astype(BF16)
                last_rows[head, j * LAST : (j + 1) * LAST, :] = whole[size - LAST :, :]

    order = [meet(own_block, i, blocks) for i in range(blocks)]
    for i in range(blocks):
        grads(i)
        if i:
            sum_levels(order[i - 1])
    gate_write = pltpu.make_async_copy(dgate_ref, dgate_out, store.at[0])
    beta_write = pltpu.make_async_copy(dbeta_ref, dbeta_out, store.at[1])
    gate_write.start()
    beta_write.start()
    for i in range(blocks // 2):
        spread_back(i)
    sum_levels(order[-1])
    for i in range(blocks // 2, blocks):
        spread_back(i)
    bodies, ends = [], []
    for j, (ref, out) in enumerate(((dq_ref, dq_out), (dk_ref, dk_out), (dv_ref, dv_out))):
        top, bottom = pl.ds(0, size - LAST), pl.ds(size - LAST, LAST)
        bodies.append(pltpu.make_async_copy(ref.at[top], out.at[top], store.at[2 + j]))
        ends.append(pltpu.make_async_copy(ref.at[bottom], out.at[bottom], store.at[5 + j]))
        bodies[-1].start()

    @pl.when(me == n - 1)
    def _():
        tail_in[...] = jnp.zeros_like(tail_in)

    for b in order:
        @pl.when(me < n - 1)
        def _():
            tail_copy(b).wait_recv()

    for head in range(heads):
        cols = slice(head * width, (head + 1) * width)
        for j, out_ref in enumerate((dq_ref, dk_ref, dv_ref)):
            rows = last_rows[head, j * LAST : (j + 1) * LAST, :]
            rows = jnp.concatenate(
                [rows[: LAST - PAD], rows[LAST - PAD :] + tail_in[head, j * PAD : (j + 1) * PAD, :]],
                0,
            )
            out_ref[size - LAST :, cols] = rows.astype(BF16)
    for copy in ends:
        copy.start()

    for b in order:
        for other in others:
            team_copy(b, other, other).wait_recv()
    for head in range(heads):
        cols = slice(head * width, (head + 1) * width)
        total = red_team[0, head]
        for i in range(1, team):
            total = total + red_team[i, head]
        for j in range(3):
            conv_ref[j, :, cols] = total[j * taps : (j + 1) * taps, :]
        decay_ref[:, cols] = total[3 * taps : 3 * taps + 1, :]

    for copy in [gate_write, beta_write] + bodies + ends:
        copy.wait()
    for other in others:
        map_copy(mine, other).wait_send()
        off_copy(0, mine, other).wait_send()
        off_copy(1, mine, other).wait_send()
        state_give(mine, other).wait_send()
        cotan_give(mine, other).wait_send()
        for b in order:
            team_copy(b, mine, other).wait_send()
    for other in other_levels:
        for b in order:
            level_copy(b, level, other).wait_send()

    @pl.when(me > 0)
    def _():
        for b in order:
            tail_copy(b).wait_send()

    @pl.when(level < levels - 1)
    def _():
        state_hop.wait_send()

    @pl.when(level > 0)
    def _():
        cotan_hop.wait_send()

    @pl.when(me < n - 1)
    def _():
        for j, ref in enumerate(raws):
            halo_copy(j, ref).wait_send()


def pack2(a, b):
    ah, al = split(a)
    bh, bl = split(b)
    return jnp.concatenate([ah, bh, al, bl], 1)


def write_kernel(count, *refs):
    sources, targets, spots = refs[:count], refs[count : 2 * count], refs[2 * count : 3 * count]
    sems = refs[-1]
    reads = [
        pltpu.make_async_copy(src, spot, sems.at[0, i])
        for i, (src, spot) in enumerate(zip(sources, spots))
    ]
    writes = [
        pltpu.make_async_copy(spot, dst, sems.at[1, i])
        for i, (spot, dst) in enumerate(zip(spots, targets))
    ]
    for copy in reads:
        copy.start()
    for i in range(count):
        reads[i].wait()
        writes[i].start()
    for copy in writes:
        copy.wait()


def per_device(query_raw, key_raw, value_raw, gate_raw, beta_raw, conv_weight, decay_log, grad_out):
    n = lax.axis_size("seq")
    size, channels = gate_raw.shape
    heads = beta_raw.shape[1]
    width = channels // heads
    group = GROUP if heads % GROUP == 0 else 1
    team = math.gcd(TEAM, math.gcd(n, heads))
    part = heads // team
    levels = n // team
    nblk = heads // group
    vmem = pl.BlockSpec(memory_space=pltpu.VMEM)
    hbm = pl.BlockSpec(memory_space=pltpu.HBM)
    act = jax.ShapeDtypeStruct((size, channels), BF16)
    shapes = (
        act, act, act,
        jax.ShapeDtypeStruct((size, channels), F32),
        jax.ShapeDtypeStruct((heads, size), F32),
        jax.ShapeDtypeStruct(conv_weight.shape, F32),
        jax.ShapeDtypeStruct((1, channels), F32),
    )

    def f32s(*shape):
        return pltpu.VMEM(shape, F32)

    def bf16s(*shape):
        return pltpu.VMEM(shape, BF16)

    def sems(*shape):
        return pltpu.SemaphoreType.DMA(shape)

    scratch = [pltpu.VMEM(x.shape, x.dtype) for x in shapes[:5]] + [
        sems(8),
        pltpu.VMEM(query_raw.shape, query_raw.dtype), pltpu.VMEM(key_raw.shape, key_raw.dtype),
        pltpu.VMEM(value_raw.shape, value_raw.dtype), pltpu.VMEM(gate_raw.shape, F32),
        f32s(heads, size), pltpu.VMEM(conv_weight.shape, F32), f32s(1, channels),
        pltpu.VMEM(grad_out.shape, grad_out.dtype), sems(8),
        f32s(heads, len(NAMES), size, width),
        bf16s(heads, 2 * size, 2 * width), bf16s(heads, size, 2 * width),
        bf16s(heads, size, 2 * width), bf16s(heads, size, 2 * width),
        bf16s(heads, 2 * size, 2 * width), bf16s(heads, size, 2 * width),
        bf16s(heads, size, 2 * size), bf16s(heads, size, 2 * width),
        f32s(heads, 8, width),
        f32s(3 * heads, PAD + size, width), f32s(3 * heads, PAD + size + PAD, width),
        pltpu.VMEM((3, PAD, channels), query_raw.dtype),
        bf16s(heads, width + 16, width), f32s(2, heads, width, width),
        bf16s(team, part, width + 16, width), f32s(2, team, part, width, width),
        f32s(team, part, width, width), f32s(team, part, width, width),
        f32s(heads, width, width), f32s(heads, width, width),
        f32s(part, width, width), f32s(part, width, width),
        f32s(part, width, width), f32s(part, width, width),
        f32s(levels, heads, RED, width), f32s(team, heads, RED, width),
        f32s(heads, 3 * PAD, width), f32s(heads, 3 * PAD, width),
        f32s(heads, 3 * LAST, width),
        sems(3), sems(3),
        sems(team), sems(team), sems(2, team), sems(2, team),
        sems(team), sems(team), sems(team), sems(team),
        pltpu.SemaphoreType.DMA, pltpu.SemaphoreType.DMA,
        pltpu.SemaphoreType.DMA, pltpu.SemaphoreType.DMA,
        sems(levels, nblk), sems(levels, nblk), sems(team, nblk), sems(team, nblk),
        sems(nblk), sems(nblk),
    ]
    results = pl.pallas_call(
        functools.partial(layer_kernel, group),
        out_shape=shapes,
        in_specs=[hbm] * 8,
        out_specs=(hbm,) * 5 + (vmem,) * 2,
        scratch_shapes=scratch,
        compiler_params=pltpu.CompilerParams(
            collective_id=0, has_side_effects=True, vmem_limit_bytes=VMEM_LIMIT
        ),
        name="layer",
    )(
        query_raw, key_raw, value_raw, gate_raw, beta_raw.T, conv_weight,
        decay_log.reshape(1, channels), grad_out,
    )
    dq, dk, dv, dgate, dbeta, conv_sum, decay_sum = pl.pallas_call(
        functools.partial(write_kernel, len(shapes)),
        out_shape=shapes,
        in_specs=[hbm] * 7,
        out_specs=(hbm,) * 7,
        scratch_shapes=[pltpu.VMEM(x.shape, x.dtype) for x in shapes] + [sems(2, 7)],
        compiler_params=pltpu.CompilerParams(vmem_limit_bytes=VMEM_LIMIT),
        name="write",
    )(*results)
    return (dq, dk, dv, dgate, dbeta.T, conv_sum, decay_sum.reshape(channels))


def solution(mesh):
    in_specs = (
        P("seq", "head"),
        P("seq", "head"),
        P("seq", "head"),
        P("seq", "head"),
        P("seq", "head"),
        P(None, None, "head"),
        P("head"),
        P("seq", "head"),
    )
    out_specs = (
        P("seq", "head"),
        P("seq", "head"),
        P("seq", "head"),
        P("seq", "head"),
        P("seq", "head"),
        P(None, None, "head"),
        P("head"),
    )
    return jax.shard_map(
        per_device, mesh=mesh, in_specs=in_specs, out_specs=out_specs, check_vma=False
    )
```

```python
import functools
import math

import jax
import jax.numpy as jnp
from jax import lax
from jax.experimental import pallas as pl
from jax.experimental.pallas import tpu as pltpu
from jax.sharding import PartitionSpec as P

F32 = jnp.float32
BF16 = jnp.bfloat16
EPS = 1e-06
PAD = 8
RED = 16
LAST = 16
GROUP = 2
TEAM = 8
VMEM_LIMIT = 64000000


def split(x):
    hi = x.astype(BF16)
    return hi, (x - hi.astype(F32)).astype(BF16)


def pack(x):
    return jnp.concatenate(split(x), 1)


def fold(out):
    n = out.shape[1] // 2
    return out[:, :n] + out[:, n:]


def dot(a, b, ta=False, tb=False):
    return lax.dot_general(
        a, b, (((0 if ta else 1,), (1 if tb else 0,)), ((), ())), preferred_element_type=F32
    )


def twice(x):
    return jnp.concatenate([x, x], 0)


def tall(x):
    n = x.shape[1] // 2
    return jnp.concatenate([x[:, :n], x[:, n:]], 0)


def cross_rows(x):
    n = x.shape[1] // 2
    hi, lo = x[:, :n], x[:, n:]
    return jnp.concatenate(
        [jnp.concatenate([hi, hi], 1), jnp.concatenate([lo, lo], 1)], 0
    )


def nn(a, b):
    return fold(dot(a, twice(b)))


def nt(a, b):
    return fold(dot(a, cross_rows(b), tb=True))


def tn(a, b):
    return fold(dot(tall(a), twice(b), ta=True))


def mm(a, b):
    return nn(pack(a), pack(b))


def ones_mm(ones, x, parts):
    rest, terms = x, []
    for _ in range(parts):
        term = rest.astype(BF16)
        terms.append(term)
        rest = rest - term.astype(F32)
    n = x.shape[1]
    out = jnp.dot(ones.astype(BF16), jnp.concatenate(terms, 1), preferred_element_type=F32)
    total = out[:, :n]
    for i in range(1, parts):
        total = total + out[:, i * n : (i + 1) * n]
    return total


def sigmoid(x):
    return 1.0 / (1.0 + jnp.exp(-x))


def softplus(x):
    return jnp.maximum(x, 0.0) + jnp.log1p(jnp.exp(-jnp.abs(x)))


def iotas(size):
    r = lax.broadcasted_iota(jnp.int32, (size, size), 0)
    c = lax.broadcasted_iota(jnp.int32, (size, size), 1)
    return r, c


def conv_pre(ext, x_ref, halo_ref, w_ref, j, cols):
    size = x_ref.shape[0]
    ext[0:PAD, :] = halo_ref[j, :, cols].astype(F32)
    ext[PAD : PAD + size, :] = x_ref[:, cols].astype(F32)
    taps = w_ref.shape[1]
    pre = None
    for i in range(taps):
        start = PAD - taps + 1 + i
        term = w_ref[j, i : i + 1, cols] * ext[start : start + size, :]
        pre = term if pre is None else pre + term
    return pre


def pick_column(ref, index):
    row = ref[pl.ds(index, 1), :]
    r, c = iotas(row.shape[1])
    return jnp.sum(jnp.where(r == c, row, 0.0), axis=1, keepdims=True)


def unit(x):
    r = lax.rsqrt(jnp.sum(x * x, axis=1, keepdims=True) + EPS)
    return x * r, r


def decays(gate, dlog):
    size = gate.shape[0]
    half = size // 2
    r, c = iotas(size)
    speed = -jnp.exp(dlog)
    ld = speed * softplus(gate)
    cum = ones_mm(jnp.where(r >= c, 1.0, 0.0), ld, 3)
    row = lax.broadcasted_iota(jnp.int32, gate.shape, 0)
    first = row < half
    mid = jnp.where(
        first, cum[half // 2 : half // 2 + 1, :], cum[half + half // 2 : half + half // 2 + 1, :]
    )
    edge = cum[half - 1 : half, :]
    last = cum[size - 1 : size, :]
    up = jnp.exp(cum - mid)
    down = jnp.exp(mid - cum)
    cross = jnp.exp(jnp.where(first, edge - cum, cum - edge))
    full = jnp.exp(cum)
    end = jnp.exp(last - cum)
    return ld, speed * sigmoid(gate), up, down, cross, full, end, jnp.exp(last)


def unit_inverses(coups):
    size = coups[0].shape[0]
    r, c = iotas(size)
    ident = jnp.where(r == c, 1.0, 0.0)
    shift = 3
    inside = (r >> shift) == (c >> shift)
    small = [jnp.where(inside, a, 0.0) for a in coups]
    p2 = [mm(a, a) for a in small]
    base = [ident - a for a in small]
    p4 = [mm(p, p) for p in p2]
    base = [x + mm(x, p) for x, p in zip(base, p2)]
    d = [x + mm(x, p) for x, p in zip(base, p4)]
    while (1 << shift) < size:
        joined = ((r >> (shift + 1)) == (c >> (shift + 1))) & ((r >> shift) != (c >> shift))
        low = [mm(jnp.where(joined, a, 0.0), x) for a, x in zip(coups, d)]
        d = [x - mm(x, y) for x, y in zip(d, low)]
        shift += 1
    return d


NAMES = (
    "q", "k", "v", "up", "down", "cross", "full", "end", "ld", "slope", "beta",
    "sq", "sk", "sv", "qr", "kr", "raw", "u", "reach",
)


def meet(start, step, count):
    if count & (count - 1):
        return lax.rem(start + step, count)
    out, bit = 0, 1
    while bit < count:
        out = out + lax.rem(start // bit + step // bit, 2) * bit
        bit *= 2
    return out


def layer_kernel(
    group,
    q_hbm, k_hbm, v_hbm, gate_hbm, beta_hbm, w_hbm, dlog_hbm, grad_hbm,
    dq_out, dk_out, dv_out, dgate_out, dbeta_out, conv_ref, decay_ref,
    dq_ref, dk_ref, dv_ref, dgate_ref, dbeta_ref, store,
    q_ref, k_ref, v_ref, gate_ref, beta_ref, w_ref, dlog_ref, grad_ref, load,
    keep, wk, ki, kd, kc, ups, crs, inv_sp, ke_sp, dend_row,
    ext, dext, halo_in,
    map_out, off_out, map_in, off_in, out_s, out_g, state_in, cotan_in,
    in_s, in_g, send_s, send_g,
    red_level, red_team, tail_out, tail_in, last_rows,
    hs, hr, ms, mr, fs, fr, ss, sr, gs, gr, cs, cr, ds, dr, ts, tr, ls, lr, es, er,
):
    n = lax.axis_size("seq")
    me = lax.axis_index("seq")
    team, part = map_in.shape[0], map_in.shape[1]
    mine = lax.rem(me, team)
    base = me - mine
    level = me // team
    levels = n // team
    mesh_id = pl.DeviceIdType.MESH
    right = lax.rem(me + 1, n)
    left = lax.rem(me + n - 1, n)
    size = q_ref.shape[0]
    half = size // 2
    heads, width = map_out.shape[0], map_out.shape[2]
    blocks = heads // group
    own_block = (mine * part) // group

    loads = [
        pltpu.make_async_copy(src, dst, load.at[i])
        for i, (src, dst) in enumerate((
            (dlog_hbm, dlog_ref), (gate_hbm, gate_ref), (q_hbm, q_ref), (k_hbm, k_ref),
            (v_hbm, v_ref), (w_hbm, w_ref), (beta_hbm, beta_ref), (grad_hbm, grad_ref),
        ))
    ]
    for copy in loads:
        copy.start()
    barrier = pltpu.get_barrier_semaphore()
    links = [base + lax.rem(mine + i, team) for i in range(1, team)]
    links += [lax.rem(me + i * team, n) for i in range(1, levels)]
    links += [right, left]
    for peer in links:
        pl.semaphore_signal(barrier, inc=1, device_id={"seq": peer}, device_id_type=mesh_id)
    def remote(src, dst, send, recv, to):
        return pltpu.make_async_remote_copy(
            src_ref=src, dst_ref=dst, send_sem=send, recv_sem=recv,
            device_id={"seq": to}, device_id_type=mesh_id,
        )

    def halo_copy(j, ref):
        return remote(
            ref.at[pl.ds(size - PAD, PAD)], halo_in.at[j], hs.at[j], hr.at[j], right
        )

    raws = (q_ref, k_ref, v_ref)

    def block(member):
        return pl.ds(member * part, part)

    def lanes(head):
        return pl.ds(pl.multiple_of(head * width, width), width)

    def map_copy(source, target):
        return remote(
            map_out.at[block(target)], map_in.at[source], ms.at[target], mr.at[source],
            base + target,
        )

    def off_copy(slot, source, target):
        return remote(
            off_out.at[slot, block(target)], off_in.at[slot, source],
            fs.at[slot, target], fr.at[slot, source], base + target,
        )

    state_slot = 1
    if levels > 1:
        state_slot = level // (levels // 2)
        if levels % 2:
            state_slot = jnp.minimum(state_slot, 1)

    def state_give(owner, member):
        return remote(
            out_s.at[member], state_in.at[block(owner)], ss.at[member], sr.at[owner],
            base + member,
        )

    def cotan_give(owner, member):
        return remote(
            out_g.at[member], cotan_in.at[block(owner)], gs.at[member], gr.at[owner],
            base + member,
        )

    state_hop = remote(send_s, in_s, cs, cr, lax.rem(me + team, n))
    cotan_hop = remote(send_g, in_g, ds, dr, lax.rem(me + n - team, n))

    def saved(head):
        spot = keep.at[head]
        return {name: spot.at[i] for i, name in enumerate(NAMES)}

    r, c = iotas(size)
    rr, cc = iotas(width)
    low = c < half

    def block_at(step):
        return meet(own_block, blocks - 1 - step, blocks)

    def prepare(step):
        for g in range(group):
            slot = step * group + g
            cols = lanes(block_at(step) * group + g)
            s = saved(slot)
            parts = decays(gate_ref[:, cols], dlog_ref[:, cols])
            for name, value in zip(
                ("ld", "slope", "up", "down", "cross", "full", "end"), parts
            ):
                s[name][...] = value
            dend_row[slot] = jnp.broadcast_to(parts[-1], (8, width))

    loads[0].wait()
    loads[1].wait()
    for step in range(blocks // 2):
        prepare(step)
    for copy in loads[2:]:
        copy.wait()
    pl.semaphore_wait(barrier, len(links))

    @pl.when(me < n - 1)
    def _():
        for j, ref in enumerate(raws):
            halo_copy(j, ref).start()

    for step in range(blocks // 2, blocks):
        prepare(step)

    @pl.when(me == 0)
    def _():
        halo_in[...] = jnp.zeros_like(halo_in)

    @pl.when(me > 0)
    def _():
        for j, ref in enumerate(raws):
            halo_copy(j, ref).wait_recv()

    def front(step):
        start = block_at(step) * group
        held = []
        for g in range(group):
            head = start + g
            slot = step * group + g
            cols = lanes(head)
            s = saved(slot)
            up, down, cross = s["up"][...], s["down"][...], s["cross"][...]
            full, end = s["full"][...], s["end"][...]
            dend = dend_row[slot, 0:1, :]
            acts = []
            for j, ref in enumerate(raws):
                pre = conv_pre(ext.at[slot * 3 + j], ref, halo_in, w_ref, j, cols)
                sig = sigmoid(pre)
                s[("sq", "sk", "sv")[j]][...] = sig * (1.0 + pre * (1.0 - sig))
                acts.append(pre * sig)
            q, qr = unit(acts[0])
            k, kr = unit(acts[1])
            v = acts[2]
            beta = jnp.broadcast_to(sigmoid(pick_column(beta_ref, head)), (size, width))
            for name, value in (
                ("q", q), ("k", k), ("v", v), ("beta", beta),
                ("qr", jnp.broadcast_to(qr, (size, width))),
                ("kr", jnp.broadcast_to(kr, (size, width))),
            ):
                s[name][...] = value
            kfull = k * full
            ups_sp = pack(jnp.concatenate([q * up, k * up], 0))
            ups[slot] = ups_sp
            kd_sp = pack(k * down)
            kd[slot] = kd_sp
            kcross = k * cross
            kc_sp = pack(kcross)
            kc[slot] = kc_sp
            crs_sp = pack(jnp.concatenate([(q * cross)[half:], kcross[half:]], 0))
            crs[slot] = crs_sp
            same = nt(ups_sp, kd_sp)
            other = nt(crs_sp, kc_sp)
            rest = size - half
            att = jnp.concatenate(
                [same[:half], jnp.where(low[half:], other[:rest], same[half:size])], 0
            )
            raw = jnp.concatenate(
                [same[size : size + half], jnp.where(low[half:], other[rest:], same[size + half :])],
                0,
            )
            att = jnp.where(r >= c, att, 0.0)
            raw = jnp.where(r > c, raw, 0.0)
            s["raw"][...] = raw
            grad = grad_ref[:, cols]
            ah, al = split(att)
            both = dot(jnp.concatenate([ah, al], 1), grad, ta=True)
            reach = both[:size] + both[size:]
            s["reach"][...] = reach
            wk[slot, size:, :] = pack(kfull)
            ke_sp[slot] = pack(k * end)
            held.append((raw * beta, beta * kfull, beta * v, pack(q * full), reach, dend))
        return held

    def back(step, held, invs):
        start = block_at(step) * group
        for g in range(group):
            head = start + g
            slot = step * group + g
            cols = lanes(head)
            s = saved(slot)
            isp = pack(invs[g])
            inv_sp[slot] = isp
            by = nn(isp, pack2(held[g][1], held[g][2]))
            s["u"][...] = by[:, width:]
            bh, bl = split(by)
            wsp = jnp.concatenate([bh[:, :width], bl[:, :width]], 1)
            wk[slot, :size, :] = wsp
            ends = tn(ke_sp[slot], jnp.concatenate([bh, bl], 1))
            full_map = jnp.where(rr == cc, held[g][5], 0.0) - ends[:, :width]
            map_hi = full_map.astype(BF16)
            left_over = jnp.sum(
                jnp.where(rr == cc, full_map - map_hi.astype(F32), 0.0), axis=0, keepdims=True
            )
            map_out[head, :width, :] = map_hi
            map_out[head, width:, :] = jnp.broadcast_to(left_over, (16, width)).astype(BF16)
            off_out[state_slot, head] = ends[:, width:]
            grad = grad_ref[:, cols]
            gsp = jnp.concatenate([grad, jnp.zeros_like(grad)], 1)
            off_out[1 - state_slot, head] = tn(
                jnp.concatenate([held[g][3], -wsp], 0),
                jnp.concatenate([gsp, pack(held[g][4])], 0),
            )
        for g in range(group):
            head = start + g
            target = head // part

            @pl.when((target != mine) & (lax.rem(head, part) == part - 1))
            def _():
                map_copy(mine, target).start()
                off_copy(0, mine, target).start()

    def send_rest(step):
        start = block_at(step) * group
        for g in range(group):
            head = start + g
            target = head // part

            @pl.when((target != mine) & (lax.rem(head, part) == part - 1))
            def _():
                off_copy(1, mine, target).start()

    held = front(0)
    for step in range(blocks):
        invs = unit_inverses([item[0] for item in held])
        back(step, held, invs)
        held = front(step + 1) if step + 1 < blocks else None
        if step:
            send_rest(step - 1)
    send_rest(blocks - 1)
    map_in[mine] = map_out[block(mine)]
    off_in[0, mine] = off_out[0, block(mine)]
    off_in[1, mine] = off_out[1, block(mine)]

    def step_maps(j, h):
        both = map_in[j, h]
        rest = jnp.where(rr == cc, both[width : width + 1, :].astype(F32), 0.0).astype(BF16)
        return both[:width], rest

    def forward_step(slot, j, h, state):
        hi, rest = step_maps(j, h)
        return nn(jnp.concatenate([hi, rest], 1), pack(state)) + off_in[slot, j, h]

    def backward_step(slot, j, h, cotan):
        hi, rest = step_maps(j, h)
        out = fold(dot(jnp.concatenate([hi, rest], 0), twice(pack(cotan)), ta=True))
        return out + off_in[slot, j, h]

    def arrive(slot, j):
        @pl.when(j != mine)
        def _():
            if slot == 0:
                map_copy(j, j).wait_recv()
            off_copy(slot, j, j).wait_recv()

    def forward(slot):
        @pl.when(level == 0)
        def _():
            in_s[...] = jnp.zeros_like(in_s)

        @pl.when(level > 0)
        def _():
            state_hop.wait_recv()

        states = [in_s[h] for h in range(part)]
        for j in range(team):
            arrive(slot, j)
            for h in range(part):
                out_s[j, h] = states[h]
                states[h] = forward_step(slot, j, h, states[h])

        @pl.when(level < levels - 1)
        def _():
            for h in range(part):
                send_s[h] = states[h]
            state_hop.start()

        state_in[block(mine)] = out_s[mine]
        for i in range(1, team):
            state_give(mine, meet(mine, i, team)).start()

    def backward(slot):
        @pl.when(level == levels - 1)
        def _():
            in_g[...] = jnp.zeros_like(in_g)

        @pl.when(level < levels - 1)
        def _():
            cotan_hop.wait_recv()

        cotans = [in_g[h] for h in range(part)]
        for j in range(team - 1, -1, -1):
            arrive(slot, j)
            for h in range(part):
                out_g[j, h] = cotans[h]
                cotans[h] = backward_step(slot, j, h, cotans[h])

        @pl.when(level > 0)
        def _():
            for h in range(part):
                send_g[h] = cotans[h]
            cotan_hop.start()

        cotan_in[block(mine)] = out_g[mine]
        for i in range(1, team):
            cotan_give(mine, meet(mine, i, team)).start()

    def ready(slot):
        s = saved(slot)
        isp = inv_sp[slot]
        rh, rl = split(s["reach"][...])
        esp = ke_sp[slot]
        rhs = jnp.concatenate([rh, esp[:, :width], rl, esp[:, width:]], 1)
        out = tn(isp, rhs)
        s["reach"][...] = out[:, :width]
        ki[slot] = pack(out[:, width:])

    @pl.when(level < levels // 2)
    def _():
        forward(0)

    @pl.when(level >= levels // 2)
    def _():
        backward(0)

    for slot in range(heads):
        ready(slot)

    @pl.when(level < levels // 2)
    def _():
        backward(1)

    @pl.when(level >= levels // 2)
    def _():
        forward(1)

    def level_copy(b, source, target):
        spot = red_level.at[source, pl.ds(b * group, group)]
        return remote(
            spot, spot, ts.at[target, b], tr.at[source, b], lax.rem(target * team + mine, n)
        )

    def team_copy(b, source, target):
        spot = red_team.at[source, pl.ds(b * group, group)]
        return remote(spot, spot, ls.at[target, b], lr.at[source, b], base + target)

    def tail_copy(b):
        spot = pl.ds(b * group, group)
        return remote(tail_out.at[spot], tail_in.at[spot], es.at[b], er.at[b], left)

    other_levels = [lax.rem(level + i, levels) for i in range(1, levels)]
    others = [meet(mine, i, team) for i in range(1, team)]
    upper = jnp.where(c >= r, 1.0, 0.0)
    ones8 = jnp.ones((8, width), BF16)
    taps = w_ref.shape[1]

    def grads(i):
        b = order[i]
        for g in range(group):
            head = b * group + g
            owner = head // part

            @pl.when((owner != mine) & (lax.rem(head, part) == 0))
            def _():
                state_give(owner, owner).wait_recv()
                cotan_give(owner, owner).wait_recv()

        for g in range(group):
            head = b * group + g
            slot = (blocks - 1 - i) * group + g
            cols = lanes(head)
            s = saved(slot)
            state, cotan = state_in[head], cotan_in[head]
            ssp, csp = pack(state), pack(cotan)
            wkx = nn(wk[slot], ssp)
            deltas = s["u"][...] - wkx[:size]
            resid = s["v"][...] - wkx[size:]
            d_err = s["reach"][...] + nn(ki[slot], csp)
            beta = s["beta"][...]
            d_v = beta * d_err
            grad = grad_ref[:, cols]
            esp = pack(d_err)
            lhs = jnp.concatenate(
                [jnp.concatenate([grad, jnp.zeros_like(grad)], 1), esp], 0
            )
            dsp = pack(deltas)
            to_full = nt(lhs, ssp)
            scores = nt(lhs, dsp)
            d_ke = nt(dsp, csp)
            d_att = jnp.where(r >= c, scores[:size], 0.0)
            d_coup = jnp.where(r > c, -scores[size:], 0.0)
            d_beta = jnp.sum(
                d_err * resid + d_coup * s["raw"][...], axis=1, keepdims=True
            )
            d_raw = d_coup * beta
            crossed = jnp.concatenate(
                [jnp.where(low[half:], d_att[half:], 0.0), jnp.where(low[half:], d_raw[half:], 0.0)],
                0,
            )
            both = jnp.concatenate(
                [
                    d_att[:half], jnp.where(low[half:], 0.0, d_att[half:]),
                    d_raw[:half], jnp.where(low[half:], 0.0, d_raw[half:]),
                ],
                0,
            )
            bsp, xsp = pack(both), pack(crossed)
            from_same = nn(bsp, kd[slot])
            from_other = nn(xsp, kc[slot])
            to_down = tn(bsp, ups[slot])
            to_cross = tn(xsp, crs[slot])
            up, cross, full, end = s["up"][...], s["cross"][...], s["full"][...], s["end"][...]
            q, k = s["q"][...], s["k"][...]
            rest = size - half
            d_q = from_same[:size] * up + to_full[:size] * full
            d_q = jnp.concatenate([d_q[:half], d_q[half:] + from_other[:rest] * cross[half:]], 0)
            d_k_up = from_same[size:] * up - (beta * to_full[size:]) * full
            d_k_up = jnp.concatenate(
                [d_k_up[:half], d_k_up[half:] + from_other[rest:] * cross[half:]], 0
            )
            k_end_part = d_ke * end
            d_k_down = to_down * s["down"][...] + k_end_part
            d_k_down = jnp.concatenate(
                [d_k_down[:half] + to_cross[:half] * cross[:half], d_k_down[half:]], 0
            )
            d_k = d_k_up + d_k_down
            d_cum = q * d_q + k * (d_k_up - d_k_down)
            end_state = fold(dot(ones8, tall(pack(state * cotan)), tb=True))[0:1, :]
            d_last = (
                jnp.sum(k * k_end_part, axis=0, keepdims=True)
                + dend_row[slot, 0:1, :] * end_state
            )
            d_ld = ones_mm(upper, d_cum, 2) + d_last
            dgate_ref[:, cols] = s["slope"][...] * d_ld
            d_dlog = jnp.sum(s["ld"][...] * d_ld, axis=0, keepdims=True)
            d_braw = d_beta * (beta * (1.0 - beta))
            dbeta_ref[pl.ds(head, 1), :] = jnp.sum(
                jnp.where(r == c, d_braw, 0.0), axis=0, keepdims=True
            )
            d_q = s["qr"][...] * (d_q - q * jnp.sum(q * d_q, axis=1, keepdims=True))
            d_k = s["kr"][...] * (d_k - k * jnp.sum(k * d_k, axis=1, keepdims=True))
            red = []
            for j, (d_act, slope) in enumerate(((d_q, "sq"), (d_k, "sk"), (d_v, "sv"))):
                d_pre = d_act * s[slope][...]
                spot = dext.at[3 * slot + j]
                spot[0:PAD, :] = jnp.zeros((PAD, width), F32)
                spot[PAD : PAD + size, :] = d_pre
                spot[PAD + size :, :] = jnp.zeros((PAD, width), F32)
                tail = None
                for tap in range(taps):
                    w = w_ref[j, tap : tap + 1, cols]
                    edge = w * spot[taps - 1 - tap : taps - 1 - tap + PAD, :]
                    tail = edge if tail is None else tail + edge
                    begin = PAD - taps + 1 + tap
                    x = ext[slot * 3 + j, begin : begin + size, :]
                    red.append(jnp.sum(d_pre * x, axis=0, keepdims=True))
                tail_out[head, j * PAD : (j + 1) * PAD, :] = tail
            red.append(d_dlog)
            red.append(jnp.zeros((RED - len(red), width), F32))
            red_level[level, head] = jnp.concatenate(red, 0)
        for other in other_levels:
            level_copy(b, level, other).start()

        @pl.when(me > 0)
        def _():
            tail_copy(b).start()

    def sum_levels(b):
        for other in other_levels:
            level_copy(b, other, other).wait_recv()
        spot = pl.ds(b * group, group)
        total = red_level[0, spot]
        for i in range(1, levels):
            total = total + red_level[i, spot]
        red_team[mine, spot] = total
        for other in others:
            team_copy(b, mine, other).start()

    def spread_back(i):
        for g in range(group):
            head = order[i] * group + g
            slot = (blocks - 1 - i) * group + g
            cols = lanes(head)
            for j, out_ref in enumerate((dq_ref, dk_ref, dv_ref)):
                spot = dext.at[3 * slot + j]
                whole = None
                for tap in range(taps):
                    start = PAD + taps - 1 - tap
                    term = w_ref[j, tap : tap + 1, cols] * spot[start : start + size, :]
                    whole = term if whole is None else whole + term
                out_ref[:, cols] = whole.astype(BF16)
                last_rows[head, j * LAST : (j + 1) * LAST, :] = whole[size - LAST :, :]

    order = [meet(own_block, i, blocks) for i in range(blocks)]
    for i in range(blocks):
        grads(i)
        if i:
            sum_levels(order[i - 1])
    gate_write = pltpu.make_async_copy(dgate_ref, dgate_out, store.at[0])
    beta_write = pltpu.make_async_copy(dbeta_ref, dbeta_out, store.at[1])
    gate_write.start()
    beta_write.start()
    for i in range(blocks // 2):
        spread_back(i)
    sum_levels(order[-1])
    for i in range(blocks // 2, blocks):
        spread_back(i)
    bodies, ends = [], []
    for j, (ref, out) in enumerate(((dq_ref, dq_out), (dk_ref, dk_out), (dv_ref, dv_out))):
        top, bottom = pl.ds(0, size - LAST), pl.ds(size - LAST, LAST)
        bodies.append(pltpu.make_async_copy(ref.at[top], out.at[top], store.at[2 + j]))
        ends.append(pltpu.make_async_copy(ref.at[bottom], out.at[bottom], store.at[5 + j]))
        bodies[-1].start()

    @pl.when(me == n - 1)
    def _():
        tail_in[...] = jnp.zeros_like(tail_in)

    for b in order:
        @pl.when(me < n - 1)
        def _():
            tail_copy(b).wait_recv()

    for head in range(heads):
        cols = slice(head * width, (head + 1) * width)
        for j, out_ref in enumerate((dq_ref, dk_ref, dv_ref)):
            rows = last_rows[head, j * LAST : (j + 1) * LAST, :]
            rows = jnp.concatenate(
                [rows[: LAST - PAD], rows[LAST - PAD :] + tail_in[head, j * PAD : (j + 1) * PAD, :]],
                0,
            )
            out_ref[size - LAST :, cols] = rows.astype(BF16)
    for copy in ends:
        copy.start()

    for b in order:
        for other in others:
            team_copy(b, other, other).wait_recv()
    for head in range(heads):
        cols = slice(head * width, (head + 1) * width)
        total = red_team[0, head]
        for i in range(1, team):
            total = total + red_team[i, head]
        for j in range(3):
            conv_ref[j, :, cols] = total[j * taps : (j + 1) * taps, :]
        decay_ref[:, cols] = total[3 * taps : 3 * taps + 1, :]

    for copy in [gate_write, beta_write] + bodies + ends:
        copy.wait()
    for other in others:
        map_copy(mine, other).wait_send()
        off_copy(0, mine, other).wait_send()
        off_copy(1, mine, other).wait_send()
        state_give(mine, other).wait_send()
        cotan_give(mine, other).wait_send()
        for b in order:
            team_copy(b, mine, other).wait_send()
    for other in other_levels:
        for b in order:
            level_copy(b, level, other).wait_send()

    @pl.when(me > 0)
    def _():
        for b in order:
            tail_copy(b).wait_send()

    @pl.when(level < levels - 1)
    def _():
        state_hop.wait_send()

    @pl.when(level > 0)
    def _():
        cotan_hop.wait_send()

    @pl.when(me < n - 1)
    def _():
        for j, ref in enumerate(raws):
            halo_copy(j, ref).wait_send()


def pack2(a, b):
    ah, al = split(a)
    bh, bl = split(b)
    return jnp.concatenate([ah, bh, al, bl], 1)


def write_kernel(count, *refs):
    sources, targets, spots = refs[:count], refs[count : 2 * count], refs[2 * count : 3 * count]
    sems = refs[-1]
    reads = [
        pltpu.make_async_copy(src, spot, sems.at[0, i])
        for i, (src, spot) in enumerate(zip(sources, spots))
    ]
    writes = [
        pltpu.make_async_copy(spot, dst, sems.at[1, i])
        for i, (spot, dst) in enumerate(zip(spots, targets))
    ]
    for copy in reads:
        copy.start()
    for i in range(count):
        reads[i].wait()
        writes[i].start()
    for copy in writes:
        copy.wait()


def per_device(query_raw, key_raw, value_raw, gate_raw, beta_raw, conv_weight, decay_log, grad_out):
    n = lax.axis_size("seq")
    size, channels = gate_raw.shape
    heads = beta_raw.shape[1]
    width = channels // heads
    group = GROUP if heads % GROUP == 0 else 1
    team = math.gcd(TEAM, math.gcd(n, heads))
    part = heads // team
    levels = n // team
    nblk = heads // group
    vmem = pl.BlockSpec(memory_space=pltpu.VMEM)
    hbm = pl.BlockSpec(memory_space=pltpu.HBM)
    act = jax.ShapeDtypeStruct((size, channels), BF16)
    shapes = (
        act, act, act,
        jax.ShapeDtypeStruct((size, channels), F32),
        jax.ShapeDtypeStruct((heads, size), F32),
        jax.ShapeDtypeStruct(conv_weight.shape, F32),
        jax.ShapeDtypeStruct((1, channels), F32),
    )

    def f32s(*shape):
        return pltpu.VMEM(shape, F32)

    def bf16s(*shape):
        return pltpu.VMEM(shape, BF16)

    def sems(*shape):
        return pltpu.SemaphoreType.DMA(shape)

    scratch = [pltpu.VMEM(x.shape, x.dtype) for x in shapes[:5]] + [
        sems(8),
        pltpu.VMEM(query_raw.shape, query_raw.dtype), pltpu.VMEM(key_raw.shape, key_raw.dtype),
        pltpu.VMEM(value_raw.shape, value_raw.dtype), pltpu.VMEM(gate_raw.shape, F32),
        f32s(heads, size), pltpu.VMEM(conv_weight.shape, F32), f32s(1, channels),
        pltpu.VMEM(grad_out.shape, grad_out.dtype), sems(8),
        f32s(heads, len(NAMES), size, width),
        bf16s(heads, 2 * size, 2 * width), bf16s(heads, size, 2 * width),
        bf16s(heads, size, 2 * width), bf16s(heads, size, 2 * width),
        bf16s(heads, 2 * size, 2 * width), bf16s(heads, size, 2 * width),
        bf16s(heads, size, 2 * size), bf16s(heads, size, 2 * width),
        f32s(heads, 8, width),
        f32s(3 * heads, PAD + size, width), f32s(3 * heads, PAD + size + PAD, width),
        pltpu.VMEM((3, PAD, channels), query_raw.dtype),
        bf16s(heads, width + 16, width), f32s(2, heads, width, width),
        bf16s(team, part, width + 16, width), f32s(2, team, part, width, width),
        f32s(team, part, width, width), f32s(team, part, width, width),
        f32s(heads, width, width), f32s(heads, width, width),
        f32s(part, width, width), f32s(part, width, width),
        f32s(part, width, width), f32s(part, width, width),
        f32s(levels, heads, RED, width), f32s(team, heads, RED, width),
        f32s(heads, 3 * PAD, width), f32s(heads, 3 * PAD, width),
        f32s(heads, 3 * LAST, width),
        sems(3), sems(3),
        sems(team), sems(team), sems(2, team), sems(2, team),
        sems(team), sems(team), sems(team), sems(team),
        pltpu.SemaphoreType.DMA, pltpu.SemaphoreType.DMA,
        pltpu.SemaphoreType.DMA, pltpu.SemaphoreType.DMA,
        sems(levels, nblk), sems(levels, nblk), sems(team, nblk), sems(team, nblk),
        sems(nblk), sems(nblk),
    ]
    results = pl.pallas_call(
        functools.partial(layer_kernel, group),
        out_shape=shapes,
        in_specs=[hbm] * 8,
        out_specs=(hbm,) * 5 + (vmem,) * 2,
        scratch_shapes=scratch,
        compiler_params=pltpu.CompilerParams(
            collective_id=0, has_side_effects=True, vmem_limit_bytes=VMEM_LIMIT
        ),
        name="layer",
    )(
        query_raw, key_raw, value_raw, gate_raw, beta_raw.T, conv_weight,
        decay_log.reshape(1, channels), grad_out,
    )
    dq, dk, dv, dgate, dbeta, conv_sum, decay_sum = pl.pallas_call(
        functools.partial(write_kernel, len(shapes)),
        out_shape=shapes,
        in_specs=[hbm] * 7,
        out_specs=(hbm,) * 7,
        scratch_shapes=[pltpu.VMEM(x.shape, x.dtype) for x in shapes] + [sems(2, 7)],
        compiler_params=pltpu.CompilerParams(vmem_limit_bytes=VMEM_LIMIT),
        name="write",
    )(*results)
    return (dq, dk, dv, dgate, dbeta.T, conv_sum, decay_sum.reshape(channels))


def solution(mesh):
    in_specs = (
        P("seq", "head"),
        P("seq", "head"),
        P("seq", "head"),
        P("seq", "head"),
        P("seq", "head"),
        P(None, None, "head"),
        P("head"),
        P("seq", "head"),
    )
    out_specs = (
        P("seq", "head"),
        P("seq", "head"),
        P("seq", "head"),
        P("seq", "head"),
        P("seq", "head"),
        P(None, None, "head"),
        P("head"),
    )
    return jax.shard_map(
        per_device, mesh=mesh, in_specs=in_specs, out_specs=out_specs, check_vma=False
    )
```

```python
import functools
import math

import jax
import jax.numpy as jnp
from jax import lax
from jax.experimental import pallas as pl
from jax.experimental.pallas import tpu as pltpu
from jax.sharding import PartitionSpec as P

F32 = jnp.float32
BF16 = jnp.bfloat16
EPS = 1e-06
PAD = 8
RED = 16
LAST = 16
GROUP = 2
TEAM = 8
VMEM_LIMIT = 64000000


def split(x):
    hi = x.astype(BF16)
    return hi, (x - hi.astype(F32)).astype(BF16)


def pack(x):
    return jnp.concatenate(split(x), 1)


def fold(out):
    n = out.shape[1] // 2
    return out[:, :n] + out[:, n:]


def dot(a, b, ta=False, tb=False):
    return lax.dot_general(
        a, b, (((0 if ta else 1,), (1 if tb else 0,)), ((), ())), preferred_element_type=F32
    )


def twice(x):
    return jnp.concatenate([x, x], 0)


def tall(x):
    n = x.shape[1] // 2
    return jnp.concatenate([x[:, :n], x[:, n:]], 0)


def cross_rows(x):
    n = x.shape[1] // 2
    hi, lo = x[:, :n], x[:, n:]
    return jnp.concatenate(
        [jnp.concatenate([hi, hi], 1), jnp.concatenate([lo, lo], 1)], 0
    )


def nn(a, b):
    return fold(dot(a, twice(b)))


def nt(a, b):
    return fold(dot(a, cross_rows(b), tb=True))


def tn(a, b):
    return fold(dot(tall(a), twice(b), ta=True))


def mm(a, b):
    return nn(pack(a), pack(b))


def ones_mm(ones, x, parts):
    rest, terms = x, []
    for _ in range(parts):
        term = rest.astype(BF16)
        terms.append(term)
        rest = rest - term.astype(F32)
    n = x.shape[1]
    out = jnp.dot(ones.astype(BF16), jnp.concatenate(terms, 1), preferred_element_type=F32)
    total = out[:, :n]
    for i in range(1, parts):
        total = total + out[:, i * n : (i + 1) * n]
    return total


def sigmoid(x):
    return 1.0 / (1.0 + jnp.exp(-x))


def softplus(x):
    return jnp.maximum(x, 0.0) + jnp.log1p(jnp.exp(-jnp.abs(x)))


def iotas(size):
    r = lax.broadcasted_iota(jnp.int32, (size, size), 0)
    c = lax.broadcasted_iota(jnp.int32, (size, size), 1)
    return r, c


def conv_pre(ext, x_ref, halo_ref, w_ref, j, cols):
    size = x_ref.shape[0]
    ext[0:PAD, :] = halo_ref[j, :, cols].astype(F32)
    ext[PAD : PAD + size, :] = x_ref[:, cols].astype(F32)
    taps = w_ref.shape[1]
    pre = None
    for i in range(taps):
        start = PAD - taps + 1 + i
        term = w_ref[j, i : i + 1, cols] * ext[start : start + size, :]
        pre = term if pre is None else pre + term
    return pre


def pick_column(ref, index):
    row = ref[pl.ds(index, 1), :]
    r, c = iotas(row.shape[1])
    return jnp.sum(jnp.where(r == c, row, 0.0), axis=1, keepdims=True)


def unit(x):
    r = lax.rsqrt(jnp.sum(x * x, axis=1, keepdims=True) + EPS)
    return x * r, r


def decays(gate, dlog):
    size = gate.shape[0]
    half = size // 2
    r, c = iotas(size)
    speed = -jnp.exp(dlog)
    ld = speed * softplus(gate)
    cum = ones_mm(jnp.where(r >= c, 1.0, 0.0), ld, 3)
    row = lax.broadcasted_iota(jnp.int32, gate.shape, 0)
    first = row < half
    mid = jnp.where(
        first, cum[half // 2 : half // 2 + 1, :], cum[half + half // 2 : half + half // 2 + 1, :]
    )
    edge = cum[half - 1 : half, :]
    last = cum[size - 1 : size, :]
    up = jnp.exp(cum - mid)
    down = jnp.exp(mid - cum)
    cross = jnp.exp(jnp.where(first, edge - cum, cum - edge))
    full = jnp.exp(cum)
    end = jnp.exp(last - cum)
    return ld, speed * sigmoid(gate), up, down, cross, full, end, jnp.exp(last)


def unit_inverses(coups):
    size = coups[0].shape[0]
    r, c = iotas(size)
    ident = jnp.where(r == c, 1.0, 0.0)
    shift = 3
    inside = (r >> shift) == (c >> shift)
    small = [jnp.where(inside, a, 0.0) for a in coups]
    p2 = [mm(a, a) for a in small]
    base = [ident - a for a in small]
    p4 = [mm(p, p) for p in p2]
    base = [x + mm(x, p) for x, p in zip(base, p2)]
    d = [x + mm(x, p) for x, p in zip(base, p4)]
    while (1 << shift) < size:
        joined = ((r >> (shift + 1)) == (c >> (shift + 1))) & ((r >> shift) != (c >> shift))
        low = [mm(jnp.where(joined, a, 0.0), x) for a, x in zip(coups, d)]
        d = [x - mm(x, y) for x, y in zip(d, low)]
        shift += 1
    return d


NAMES = (
    "q", "k", "v", "up", "down", "cross", "full", "end", "ld", "slope", "beta",
    "sq", "sk", "sv", "qr", "kr", "raw", "u", "reach",
)


def meet(start, step, count):
    if count & (count - 1):
        return lax.rem(start + step, count)
    out, bit = 0, 1
    while bit < count:
        out = out + lax.rem(start // bit + step // bit, 2) * bit
        bit *= 2
    return out


def layer_kernel(
    group,
    q_hbm, k_hbm, v_hbm, gate_hbm, beta_hbm, w_hbm, dlog_hbm, grad_hbm,
    dq_out, dk_out, dv_out, dgate_out, dbeta_out, conv_ref, decay_ref,
    dq_ref, dk_ref, dv_ref, dgate_ref, dbeta_ref, store,
    q_ref, k_ref, v_ref, gate_ref, beta_ref, w_ref, dlog_ref, grad_ref, load,
    keep, wk, ki, kd, kc, ups, crs, inv_sp, ke_sp, dend_row,
    ext, dext, halo_in,
    map_out, off_out, map_in, off_in, out_s, out_g, state_in, cotan_in,
    in_s, in_g, send_s, send_g,
    red_level, red_team, tail_out, tail_in, last_rows,
    hs, hr, ms, mr, fs, fr, ss, sr, gs, gr, cs, cr, ds, dr, ts, tr, ls, lr, es, er,
):
    n = lax.axis_size("seq")
    me = lax.axis_index("seq")
    team, part = map_in.shape[0], map_in.shape[1]
    mine = lax.rem(me, team)
    base = me - mine
    level = me // team
    levels = n // team
    mesh_id = pl.DeviceIdType.MESH
    right = lax.rem(me + 1, n)
    left = lax.rem(me + n - 1, n)
    size = q_ref.shape[0]
    half = size // 2
    heads, width = map_out.shape[0], map_out.shape[2]
    blocks = heads // group
    own_block = (mine * part) // group

    loads = [
        pltpu.make_async_copy(src, dst, load.at[i])
        for i, (src, dst) in enumerate((
            (dlog_hbm, dlog_ref), (gate_hbm, gate_ref), (q_hbm, q_ref), (k_hbm, k_ref),
            (v_hbm, v_ref), (w_hbm, w_ref), (beta_hbm, beta_ref), (grad_hbm, grad_ref),
        ))
    ]
    for copy in loads:
        copy.start()
    barrier = pltpu.get_barrier_semaphore()
    links = [base + lax.rem(mine + i, team) for i in range(1, team)]
    links += [lax.rem(me + i * team, n) for i in range(1, levels)]
    links += [right, left]
    for peer in links:
        pl.semaphore_signal(barrier, inc=1, device_id={"seq": peer}, device_id_type=mesh_id)
    def remote(src, dst, send, recv, to):
        return pltpu.make_async_remote_copy(
            src_ref=src, dst_ref=dst, send_sem=send, recv_sem=recv,
            device_id={"seq": to}, device_id_type=mesh_id,
        )

    def halo_copy(j, ref):
        return remote(
            ref.at[pl.ds(size - PAD, PAD)], halo_in.at[j], hs.at[j], hr.at[j], right
        )

    raws = (q_ref, k_ref, v_ref)

    def block(member):
        return pl.ds(member * part, part)

    def lanes(head):
        return pl.ds(pl.multiple_of(head * width, width), width)

    def map_copy(source, target):
        return remote(
            map_out.at[block(target)], map_in.at[source], ms.at[target], mr.at[source],
            base + target,
        )

    def off_copy(slot, source, target):
        return remote(
            off_out.at[slot, block(target)], off_in.at[slot, source],
            fs.at[slot, target], fr.at[slot, source], base + target,
        )

    state_slot = 1
    if levels > 1:
        state_slot = level // (levels // 2)
        if levels % 2:
            state_slot = jnp.minimum(state_slot, 1)

    def state_give(owner, member):
        return remote(
            out_s.at[member], state_in.at[block(owner)], ss.at[member], sr.at[owner],
            base + member,
        )

    def cotan_give(owner, member):
        return remote(
            out_g.at[member], cotan_in.at[block(owner)], gs.at[member], gr.at[owner],
            base + member,
        )

    state_hop = remote(send_s, in_s, cs, cr, lax.rem(me + team, n))
    cotan_hop = remote(send_g, in_g, ds, dr, lax.rem(me + n - team, n))

    def saved(head):
        spot = keep.at[head]
        return {name: spot.at[i] for i, name in enumerate(NAMES)}

    r, c = iotas(size)
    rr, cc = iotas(width)
    low = c < half

    def block_at(step):
        return meet(own_block, blocks - 1 - step, blocks)

    def prepare(step):
        for g in range(group):
            slot = step * group + g
            cols = lanes(block_at(step) * group + g)
            s = saved(slot)
            parts = decays(gate_ref[:, cols], dlog_ref[:, cols])
            for name, value in zip(
                ("ld", "slope", "up", "down", "cross", "full", "end"), parts
            ):
                s[name][...] = value
            dend_row[slot] = jnp.broadcast_to(parts[-1], (8, width))

    loads[0].wait()
    loads[1].wait()
    for step in range(blocks // 2):
        prepare(step)
    for copy in loads[2:]:
        copy.wait()
    pl.semaphore_wait(barrier, len(links))

    @pl.when(me < n - 1)
    def _():
        for j, ref in enumerate(raws):
            halo_copy(j, ref).start()

    for step in range(blocks // 2, blocks):
        prepare(step)

    @pl.when(me == 0)
    def _():
        halo_in[...] = jnp.zeros_like(halo_in)

    @pl.when(me > 0)
    def _():
        for j, ref in enumerate(raws):
            halo_copy(j, ref).wait_recv()

    def front(step):
        start = block_at(step) * group
        held = []
        for g in range(group):
            head = start + g
            slot = step * group + g
            cols = lanes(head)
            s = saved(slot)
            up, down, cross = s["up"][...], s["down"][...], s["cross"][...]
            full, end = s["full"][...], s["end"][...]
            dend = dend_row[slot, 0:1, :]
            acts = []
            for j, ref in enumerate(raws):
                pre = conv_pre(ext.at[slot * 3 + j], ref, halo_in, w_ref, j, cols)
                sig = sigmoid(pre)
                s[("sq", "sk", "sv")[j]][...] = sig * (1.0 + pre * (1.0 - sig))
                acts.append(pre * sig)
            q, qr = unit(acts[0])
            k, kr = unit(acts[1])
            v = acts[2]
            beta = jnp.broadcast_to(sigmoid(pick_column(beta_ref, head)), (size, width))
            for name, value in (
                ("q", q), ("k", k), ("v", v), ("beta", beta),
                ("qr", jnp.broadcast_to(qr, (size, width))),
                ("kr", jnp.broadcast_to(kr, (size, width))),
            ):
                s[name][...] = value
            kfull = k * full
            ups_sp = pack(jnp.concatenate([q * up, k * up], 0))
            ups[slot] = ups_sp
            kd_sp = pack(k * down)
            kd[slot] = kd_sp
            kcross = k * cross
            kc_sp = pack(kcross)
            kc[slot] = kc_sp
            crs_sp = pack(jnp.concatenate([(q * cross)[half:], kcross[half:]], 0))
            crs[slot] = crs_sp
            same = nt(ups_sp, kd_sp)
            other = nt(crs_sp, kc_sp)
            rest = size - half
            att = jnp.concatenate(
                [same[:half], jnp.where(low[half:], other[:rest], same[half:size])], 0
            )
            raw = jnp.concatenate(
                [same[size : size + half], jnp.where(low[half:], other[rest:], same[size + half :])],
                0,
            )
            att = jnp.where(r >= c, att, 0.0)
            raw = jnp.where(r > c, raw, 0.0)
            s["raw"][...] = raw
            grad = grad_ref[:, cols]
            ah, al = split(att)
            both = dot(jnp.concatenate([ah, al], 1), grad, ta=True)
            reach = both[:size] + both[size:]
            s["reach"][...] = reach
            wk[slot, size:, :] = pack(kfull)
            ke_sp[slot] = pack(k * end)
            held.append((raw * beta, beta * kfull, beta * v, pack(q * full), reach, dend))
        return held

    def back(step, held, invs):
        start = block_at(step) * group
        for g in range(group):
            head = start + g
            slot = step * group + g
            cols = lanes(head)
            s = saved(slot)
            isp = pack(invs[g])
            inv_sp[slot] = isp
            by = nn(isp, pack2(held[g][1], held[g][2]))
            s["u"][...] = by[:, width:]
            bh, bl = split(by)
            wsp = jnp.concatenate([bh[:, :width], bl[:, :width]], 1)
            wk[slot, :size, :] = wsp
            ends = tn(ke_sp[slot], jnp.concatenate([bh, bl], 1))
            full_map = jnp.where(rr == cc, held[g][5], 0.0) - ends[:, :width]
            map_hi = full_map.astype(BF16)
            left_over = jnp.sum(
                jnp.where(rr == cc, full_map - map_hi.astype(F32), 0.0), axis=0, keepdims=True
            )
            map_out[head, :width, :] = map_hi
            map_out[head, width:, :] = jnp.broadcast_to(left_over, (16, width)).astype(BF16)
            off_out[state_slot, head] = ends[:, width:]
            grad = grad_ref[:, cols]
            gsp = jnp.concatenate([grad, jnp.zeros_like(grad)], 1)
            off_out[1 - state_slot, head] = tn(
                jnp.concatenate([held[g][3], -wsp], 0),
                jnp.concatenate([gsp, pack(held[g][4])], 0),
            )
        for g in range(group):
            head = start + g
            target = head // part

            @pl.when((target != mine) & (lax.rem(head, part) == part - 1))
            def _():
                map_copy(mine, target).start()
                off_copy(0, mine, target).start()

    def send_rest(step):
        start = block_at(step) * group
        for g in range(group):
            head = start + g
            target = head // part

            @pl.when((target != mine) & (lax.rem(head, part) == part - 1))
            def _():
                off_copy(1, mine, target).start()

    held = front(0)
    for step in range(blocks):
        invs = unit_inverses([item[0] for item in held])
        back(step, held, invs)
        held = front(step + 1) if step + 1 < blocks else None
        if step:
            send_rest(step - 1)
    send_rest(blocks - 1)
    map_in[mine] = map_out[block(mine)]
    off_in[0, mine] = off_out[0, block(mine)]
    off_in[1, mine] = off_out[1, block(mine)]

    def step_maps(j, h):
        both = map_in[j, h]
        rest = jnp.where(rr == cc, both[width : width + 1, :].astype(F32), 0.0).astype(BF16)
        return both[:width], rest

    def forward_step(slot, j, h, state):
        hi, rest = step_maps(j, h)
        return nn(jnp.concatenate([hi, rest], 1), pack(state)) + off_in[slot, j, h]

    def backward_step(slot, j, h, cotan):
        hi, rest = step_maps(j, h)
        out = fold(dot(jnp.concatenate([hi, rest], 0), twice(pack(cotan)), ta=True))
        return out + off_in[slot, j, h]

    def arrive(slot, j):
        @pl.when(j != mine)
        def _():
            if slot == 0:
                map_copy(j, j).wait_recv()
            off_copy(slot, j, j).wait_recv()

    def forward(slot):
        @pl.when(level == 0)
        def _():
            in_s[...] = jnp.zeros_like(in_s)

        @pl.when(level > 0)
        def _():
            state_hop.wait_recv()

        states = [in_s[h] for h in range(part)]
        for j in range(team):
            arrive(slot, j)
            for h in range(part):
                out_s[j, h] = states[h]
                states[h] = forward_step(slot, j, h, states[h])

        @pl.when(level < levels - 1)
        def _():
            for h in range(part):
                send_s[h] = states[h]
            state_hop.start()

        state_in[block(mine)] = out_s[mine]
        for i in range(1, team):
            state_give(mine, meet(mine, i, team)).start()

    def backward(slot):
        @pl.when(level == levels - 1)
        def _():
            in_g[...] = jnp.zeros_like(in_g)

        @pl.when(level < levels - 1)
        def _():
            cotan_hop.wait_recv()

        cotans = [in_g[h] for h in range(part)]
        for j in range(team - 1, -1, -1):
            arrive(slot, j)
            for h in range(part):
                out_g[j, h] = cotans[h]
                cotans[h] = backward_step(slot, j, h, cotans[h])

        @pl.when(level > 0)
        def _():
            for h in range(part):
                send_g[h] = cotans[h]
            cotan_hop.start()

        cotan_in[block(mine)] = out_g[mine]
        for i in range(1, team):
            cotan_give(mine, meet(mine, i, team)).start()

    def ready(slot):
        s = saved(slot)
        isp = inv_sp[slot]
        rh, rl = split(s["reach"][...])
        esp = ke_sp[slot]
        rhs = jnp.concatenate([rh, esp[:, :width], rl, esp[:, width:]], 1)
        out = tn(isp, rhs)
        s["reach"][...] = out[:, :width]
        ki[slot] = pack(out[:, width:])

    @pl.when(level < levels // 2)
    def _():
        forward(0)

    @pl.when(level >= levels // 2)
    def _():
        backward(0)

    for slot in range(heads):
        ready(slot)

    @pl.when(level < levels // 2)
    def _():
        backward(1)

    @pl.when(level >= levels // 2)
    def _():
        forward(1)

    def level_copy(b, source, target):
        spot = red_level.at[source, pl.ds(b * group, group)]
        return remote(
            spot, spot, ts.at[target, b], tr.at[source, b], lax.rem(target * team + mine, n)
        )

    def team_copy(b, source, target):
        spot = red_team.at[source, pl.ds(b * group, group)]
        return remote(spot, spot, ls.at[target, b], lr.at[source, b], base + target)

    def tail_copy(b):
        spot = pl.ds(b * group, group)
        return remote(tail_out.at[spot], tail_in.at[spot], es.at[b], er.at[b], left)

    other_levels = [lax.rem(level + i, levels) for i in range(1, levels)]
    others = [meet(mine, i, team) for i in range(1, team)]
    upper = jnp.where(c >= r, 1.0, 0.0)
    ones8 = jnp.ones((8, width), BF16)
    taps = w_ref.shape[1]

    def grads(i):
        b = order[i]
        for g in range(group):
            head = b * group + g
            owner = head // part

            @pl.when((owner != mine) & (lax.rem(head, part) == 0))
            def _():
                state_give(owner, owner).wait_recv()
                cotan_give(owner, owner).wait_recv()

        for g in range(group):
            head = b * group + g
            slot = (blocks - 1 - i) * group + g
            cols = lanes(head)
            s = saved(slot)
            state, cotan = state_in[head], cotan_in[head]
            ssp, csp = pack(state), pack(cotan)
            wkx = nn(wk[slot], ssp)
            deltas = s["u"][...] - wkx[:size]
            resid = s["v"][...] - wkx[size:]
            d_err = s["reach"][...] + nn(ki[slot], csp)
            beta = s["beta"][...]
            d_v = beta * d_err
            grad = grad_ref[:, cols]
            esp = pack(d_err)
            lhs = jnp.concatenate(
                [jnp.concatenate([grad, jnp.zeros_like(grad)], 1), esp], 0
            )
            dsp = pack(deltas)
            to_full = nt(lhs, ssp)
            scores = nt(lhs, dsp)
            d_ke = nt(dsp, csp)
            d_att = jnp.where(r >= c, scores[:size], 0.0)
            d_coup = jnp.where(r > c, -scores[size:], 0.0)
            d_beta = jnp.sum(
                d_err * resid + d_coup * s["raw"][...], axis=1, keepdims=True
            )
            d_raw = d_coup * beta
            crossed = jnp.concatenate(
                [jnp.where(low[half:], d_att[half:], 0.0), jnp.where(low[half:], d_raw[half:], 0.0)],
                0,
            )
            both = jnp.concatenate(
                [
                    d_att[:half], jnp.where(low[half:], 0.0, d_att[half:]),
                    d_raw[:half], jnp.where(low[half:], 0.0, d_raw[half:]),
                ],
                0,
            )
            bsp, xsp = pack(both), pack(crossed)
            from_same = nn(bsp, kd[slot])
            from_other = nn(xsp, kc[slot])
            to_down = tn(bsp, ups[slot])
            to_cross = tn(xsp, crs[slot])
            up, cross, full, end = s["up"][...], s["cross"][...], s["full"][...], s["end"][...]
            q, k = s["q"][...], s["k"][...]
            rest = size - half
            d_q = from_same[:size] * up + to_full[:size] * full
            d_q = jnp.concatenate([d_q[:half], d_q[half:] + from_other[:rest] * cross[half:]], 0)
            d_k_up = from_same[size:] * up - (beta * to_full[size:]) * full
            d_k_up = jnp.concatenate(
                [d_k_up[:half], d_k_up[half:] + from_other[rest:] * cross[half:]], 0
            )
            k_end_part = d_ke * end
            d_k_down = to_down * s["down"][...] + k_end_part
            d_k_down = jnp.concatenate(
                [d_k_down[:half] + to_cross[:half] * cross[:half], d_k_down[half:]], 0
            )
            d_k = d_k_up + d_k_down
            d_cum = q * d_q + k * (d_k_up - d_k_down)
            end_state = fold(dot(ones8, tall(pack(state * cotan)), tb=True))[0:1, :]
            d_last = (
                jnp.sum(k * k_end_part, axis=0, keepdims=True)
                + dend_row[slot, 0:1, :] * end_state
            )
            d_ld = ones_mm(upper, d_cum, 2) + d_last
            dgate_ref[:, cols] = s["slope"][...] * d_ld
            d_dlog = jnp.sum(s["ld"][...] * d_ld, axis=0, keepdims=True)
            d_braw = d_beta * (beta * (1.0 - beta))
            dbeta_ref[pl.ds(head, 1), :] = jnp.sum(
                jnp.where(r == c, d_braw, 0.0), axis=0, keepdims=True
            )
            d_q = s["qr"][...] * (d_q - q * jnp.sum(q * d_q, axis=1, keepdims=True))
            d_k = s["kr"][...] * (d_k - k * jnp.sum(k * d_k, axis=1, keepdims=True))
            red = []
            for j, (d_act, slope) in enumerate(((d_q, "sq"), (d_k, "sk"), (d_v, "sv"))):
                d_pre = d_act * s[slope][...]
                spot = dext.at[3 * slot + j]
                spot[0:PAD, :] = jnp.zeros((PAD, width), F32)
                spot[PAD : PAD + size, :] = d_pre
                spot[PAD + size :, :] = jnp.zeros((PAD, width), F32)
                tail = None
                for tap in range(taps):
                    w = w_ref[j, tap : tap + 1, cols]
                    edge = w * spot[taps - 1 - tap : taps - 1 - tap + PAD, :]
                    tail = edge if tail is None else tail + edge
                    begin = PAD - taps + 1 + tap
                    x = ext[slot * 3 + j, begin : begin + size, :]
                    red.append(jnp.sum(d_pre * x, axis=0, keepdims=True))
                tail_out[head, j * PAD : (j + 1) * PAD, :] = tail
            red.append(d_dlog)
            red.append(jnp.zeros((RED - len(red), width), F32))
            red_level[level, head] = jnp.concatenate(red, 0)
        for other in other_levels:
            level_copy(b, level, other).start()

        @pl.when(me > 0)
        def _():
            tail_copy(b).start()

    def sum_levels(b):
        for other in other_levels:
            level_copy(b, other, other).wait_recv()
        spot = pl.ds(b * group, group)
        total = red_level[0, spot]
        for i in range(1, levels):
            total = total + red_level[i, spot]
        red_team[mine, spot] = total
        for other in others:
            team_copy(b, mine, other).start()

    def spread_back(i):
        for g in range(group):
            head = order[i] * group + g
            slot = (blocks - 1 - i) * group + g
            cols = lanes(head)
            for j, out_ref in enumerate((dq_ref, dk_ref, dv_ref)):
                spot = dext.at[3 * slot + j]
                whole = None
                for tap in range(taps):
                    start = PAD + taps - 1 - tap
                    term = w_ref[j, tap : tap + 1, cols] * spot[start : start + size, :]
                    whole = term if whole is None else whole + term
                out_ref[:, cols] = whole.astype(BF16)
                last_rows[head, j * LAST : (j + 1) * LAST, :] = whole[size - LAST :, :]

    order = [meet(own_block, i, blocks) for i in range(blocks)]
    for i in range(blocks):
        grads(i)
        if i:
            sum_levels(order[i - 1])
    gate_write = pltpu.make_async_copy(dgate_ref, dgate_out, store.at[0])
    beta_write = pltpu.make_async_copy(dbeta_ref, dbeta_out, store.at[1])
    gate_write.start()
    beta_write.start()
    sum_levels(order[-1])
    for i in range(blocks):
        spread_back(i)
    bodies, ends = [], []
    for j, (ref, out) in enumerate(((dq_ref, dq_out), (dk_ref, dk_out), (dv_ref, dv_out))):
        top, bottom = pl.ds(0, size - LAST), pl.ds(size - LAST, LAST)
        bodies.append(pltpu.make_async_copy(ref.at[top], out.at[top], store.at[2 + j]))
        ends.append(pltpu.make_async_copy(ref.at[bottom], out.at[bottom], store.at[5 + j]))
        bodies[-1].start()

    @pl.when(me == n - 1)
    def _():
        tail_in[...] = jnp.zeros_like(tail_in)

    for b in order:
        @pl.when(me < n - 1)
        def _():
            tail_copy(b).wait_recv()

    for head in range(heads):
        cols = slice(head * width, (head + 1) * width)
        for j, out_ref in enumerate((dq_ref, dk_ref, dv_ref)):
            rows = last_rows[head, j * LAST : (j + 1) * LAST, :]
            rows = jnp.concatenate(
                [rows[: LAST - PAD], rows[LAST - PAD :] + tail_in[head, j * PAD : (j + 1) * PAD, :]],
                0,
            )
            out_ref[size - LAST :, cols] = rows.astype(BF16)
    for copy in ends:
        copy.start()

    for b in order:
        for other in others:
            team_copy(b, other, other).wait_recv()
    for head in range(heads):
        cols = slice(head * width, (head + 1) * width)
        total = red_team[0, head]
        for i in range(1, team):
            total = total + red_team[i, head]
        for j in range(3):
            conv_ref[j, :, cols] = total[j * taps : (j + 1) * taps, :]
        decay_ref[:, cols] = total[3 * taps : 3 * taps + 1, :]

    for copy in [gate_write, beta_write] + bodies + ends:
        copy.wait()
    for other in others:
        map_copy(mine, other).wait_send()
        off_copy(0, mine, other).wait_send()
        off_copy(1, mine, other).wait_send()
        state_give(mine, other).wait_send()
        cotan_give(mine, other).wait_send()
        for b in order:
            team_copy(b, mine, other).wait_send()
    for other in other_levels:
        for b in order:
            level_copy(b, level, other).wait_send()

    @pl.when(me > 0)
    def _():
        for b in order:
            tail_copy(b).wait_send()

    @pl.when(level < levels - 1)
    def _():
        state_hop.wait_send()

    @pl.when(level > 0)
    def _():
        cotan_hop.wait_send()

    @pl.when(me < n - 1)
    def _():
        for j, ref in enumerate(raws):
            halo_copy(j, ref).wait_send()


def pack2(a, b):
    ah, al = split(a)
    bh, bl = split(b)
    return jnp.concatenate([ah, bh, al, bl], 1)


def write_kernel(count, *refs):
    sources, targets, spots = refs[:count], refs[count : 2 * count], refs[2 * count : 3 * count]
    sems = refs[-1]
    reads = [
        pltpu.make_async_copy(src, spot, sems.at[0, i])
        for i, (src, spot) in enumerate(zip(sources, spots))
    ]
    writes = [
        pltpu.make_async_copy(spot, dst, sems.at[1, i])
        for i, (spot, dst) in enumerate(zip(spots, targets))
    ]
    for copy in reads:
        copy.start()
    for i in range(count):
        reads[i].wait()
        writes[i].start()
    for copy in writes:
        copy.wait()


def per_device(query_raw, key_raw, value_raw, gate_raw, beta_raw, conv_weight, decay_log, grad_out):
    n = lax.axis_size("seq")
    size, channels = gate_raw.shape
    heads = beta_raw.shape[1]
    width = channels // heads
    group = GROUP if heads % GROUP == 0 else 1
    team = math.gcd(TEAM, math.gcd(n, heads))
    part = heads // team
    levels = n // team
    nblk = heads // group
    vmem = pl.BlockSpec(memory_space=pltpu.VMEM)
    hbm = pl.BlockSpec(memory_space=pltpu.HBM)
    act = jax.ShapeDtypeStruct((size, channels), BF16)
    shapes = (
        act, act, act,
        jax.ShapeDtypeStruct((size, channels), F32),
        jax.ShapeDtypeStruct((heads, size), F32),
        jax.ShapeDtypeStruct(conv_weight.shape, F32),
        jax.ShapeDtypeStruct((1, channels), F32),
    )

    def f32s(*shape):
        return pltpu.VMEM(shape, F32)

    def bf16s(*shape):
        return pltpu.VMEM(shape, BF16)

    def sems(*shape):
        return pltpu.SemaphoreType.DMA(shape)

    scratch = [pltpu.VMEM(x.shape, x.dtype) for x in shapes[:5]] + [
        sems(8),
        pltpu.VMEM(query_raw.shape, query_raw.dtype), pltpu.VMEM(key_raw.shape, key_raw.dtype),
        pltpu.VMEM(value_raw.shape, value_raw.dtype), pltpu.VMEM(gate_raw.shape, F32),
        f32s(heads, size), pltpu.VMEM(conv_weight.shape, F32), f32s(1, channels),
        pltpu.VMEM(grad_out.shape, grad_out.dtype), sems(8),
        f32s(heads, len(NAMES), size, width),
        bf16s(heads, 2 * size, 2 * width), bf16s(heads, size, 2 * width),
        bf16s(heads, size, 2 * width), bf16s(heads, size, 2 * width),
        bf16s(heads, 2 * size, 2 * width), bf16s(heads, size, 2 * width),
        bf16s(heads, size, 2 * size), bf16s(heads, size, 2 * width),
        f32s(heads, 8, width),
        f32s(3 * heads, PAD + size, width), f32s(3 * heads, PAD + size + PAD, width),
        pltpu.VMEM((3, PAD, channels), query_raw.dtype),
        bf16s(heads, width + 16, width), f32s(2, heads, width, width),
        bf16s(team, part, width + 16, width), f32s(2, team, part, width, width),
        f32s(team, part, width, width), f32s(team, part, width, width),
        f32s(heads, width, width), f32s(heads, width, width),
        f32s(part, width, width), f32s(part, width, width),
        f32s(part, width, width), f32s(part, width, width),
        f32s(levels, heads, RED, width), f32s(team, heads, RED, width),
        f32s(heads, 3 * PAD, width), f32s(heads, 3 * PAD, width),
        f32s(heads, 3 * LAST, width),
        sems(3), sems(3),
        sems(team), sems(team), sems(2, team), sems(2, team),
        sems(team), sems(team), sems(team), sems(team),
        pltpu.SemaphoreType.DMA, pltpu.SemaphoreType.DMA,
        pltpu.SemaphoreType.DMA, pltpu.SemaphoreType.DMA,
        sems(levels, nblk), sems(levels, nblk), sems(team, nblk), sems(team, nblk),
        sems(nblk), sems(nblk),
    ]
    results = pl.pallas_call(
        functools.partial(layer_kernel, group),
        out_shape=shapes,
        in_specs=[hbm] * 8,
        out_specs=(hbm,) * 5 + (vmem,) * 2,
        scratch_shapes=scratch,
        compiler_params=pltpu.CompilerParams(
            collective_id=0, has_side_effects=True, vmem_limit_bytes=VMEM_LIMIT
        ),
        name="layer",
    )(
        query_raw, key_raw, value_raw, gate_raw, beta_raw.T, conv_weight,
        decay_log.reshape(1, channels), grad_out,
    )
    dq, dk, dv, dgate, dbeta, conv_sum, decay_sum = pl.pallas_call(
        functools.partial(write_kernel, len(shapes)),
        out_shape=shapes,
        in_specs=[hbm] * 7,
        out_specs=(hbm,) * 7,
        scratch_shapes=[pltpu.VMEM(x.shape, x.dtype) for x in shapes] + [sems(2, 7)],
        compiler_params=pltpu.CompilerParams(vmem_limit_bytes=VMEM_LIMIT),
        name="write",
    )(*results)
    return (dq, dk, dv, dgate, dbeta.T, conv_sum, decay_sum.reshape(channels))


def solution(mesh):
    in_specs = (
        P("seq", "head"),
        P("seq", "head"),
        P("seq", "head"),
        P("seq", "head"),
        P("seq", "head"),
        P(None, None, "head"),
        P("head"),
        P("seq", "head"),
    )
    out_specs = (
        P("seq", "head"),
        P("seq", "head"),
        P("seq", "head"),
        P("seq", "head"),
        P("seq", "head"),
        P(None, None, "head"),
        P("head"),
    )
    return jax.shard_map(
        per_device, mesh=mesh, in_specs=in_specs, out_specs=out_specs, check_vma=False
    )
```
